256 devices in a mesh: row: 8 (over x_hi, y), col: 16 (over x_lo, z), depth: 2 (over core).
Axes of the slice: x: 4 (x_hi: 2, x_lo: 2; x = x_hi * 2 + x_lo), y: 4, z: 8, core: 2. Of those that a mesh axis runs over, the one named last changes fastest.
Arguments:
- snapshots: bfloat16 [8192, 6144], P('col', ('row', 'depth')), may hold values from -6 to 6
- cell_weight: float32 [6144], P(('row', 'depth')), may hold values from 0.25 to 4
Outputs:
- gram: float32 [8192, 8192], P('row', ('col', 'depth'))
The draws below stay inside these ranges and needn't reach their ends.
All inputs are finite; a program needn't handle non-finite values.
Results may differ from the reference program's by a relative error of at most 0.0034.
Values may be sent and summed in bfloat16 or wider, within the bound.
A program may use at most 64 MiB of HBM per device.

```python
import math
import jax
import jax.numpy as jnp
from jax import lax

SNAPS = 8192
CELLS = 6144


def block_levels(key, dims, pieces, least, high):
    def one(position, parts):
        draws = jax.random.uniform(jax.random.fold_in(jax.random.fold_in(key, 6), position), (parts,), jnp.float32, least / len(pieces), high / len(pieces))
        return jnp.repeat(jnp.exp(draws), dims[position] // parts).reshape((-1,) + (1,) * (len(dims) - position - 1))

    gain = one(*pieces[0])
    for cut in pieces[1:]:
        gain = gain * one(*cut)
    return gain


def scatter_about(own_key, extent, spread, reach, pieces=(), held_as=jnp.bfloat16):
    level = block_levels(own_key, extent, pieces, -0.22, 0.18) if pieces else 1.0
    result = jax.random.normal(own_key, extent, jnp.float32) * spread * level
    return jnp.minimum(jnp.maximum(result, -reach), reach).astype(held_as)


def setup_inputs(seed: int = 0) -> dict:
    seeds = jax.random.split(jax.random.key(seed), 3)
    return {
        "snapshots": scatter_about(seeds[0], (SNAPS, CELLS), 1.0, 6.0, ((0, 16), (1, 16))),
        "cell_weight": jnp.clip(jnp.exp(math.log(4.0) - 2.7725887 * jax.random.uniform(seeds[1], (CELLS,), jnp.float32) ** block_levels(seeds[1], (CELLS,), ((0, 16),), -0.2, 0.2)), 0.25, 4.0),
    }


def reference(snapshots, cell_weight):
    root_weight = jnp.sqrt(cell_weight.astype(jnp.float32))
    scaled = (snapshots.astype(jnp.float32) * root_weight[None, :]).astype(jnp.bfloat16)
    total = lax.dot_general(scaled, scaled, (((1,), (1,)), ((), ())), preferred_element_type=jnp.float32)
    return total / jnp.float32(CELLS)
```

```python
import functools

import jax
import jax.numpy as jnp
from jax import lax
from jax.experimental import pallas as pl
from jax.experimental.pallas import tpu as pltpu
from jax.sharding import PartitionSpec as P

MESH = pl.DeviceIdType.MESH
CELLS = 6144
SNAP = 512
CELL = 384
PART = 64
COLS = 256


def kernel(
    snap_ref, weight_ref, out_ref, own, cols, rows, partial, peer, half_out, half_in,
    a_send, a_recv, x_send, x_recv, y_send, y_recv, f_send, f_recv,
    z_send, z_recv, p_send, p_recv, q_send, q_recv,
):
    row, col, d = lax.axis_index("row"), lax.axis_index("col"), lax.axis_index("depth")
    h, y, l, z = row // 4, lax.rem(row, 4), col // 8, lax.rem(col, 8)

    def device(h, l, y, z, d):
        return (h * 4 + y, l * 8 + z, d)

    def turn(value, by, size):
        return lax.rem(value + by + size, size)

    up_y, down_y = device(h, l, turn(y, 1, 4), z, d), device(h, l, turn(y, -1, 4), z, d)
    up_z, down_z = device(h, l, y, turn(z, 1, 8), d), device(h, l, y, turn(z, -1, 8), d)
    sibling = device(h, l, y, z, 1 - d)
    partner = device(h, 1 - l, y, z, d)

    barrier = pltpu.get_barrier_semaphore()

    def greet(target):
        pl.semaphore_signal(barrier, inc=1, device_id=target, device_id_type=MESH)

    for target in (up_y, down_y, up_z, down_z, sibling, partner):
        greet(target)
    for block in range(2):
        greet(device(l, block, y, z, d))
        for part_y in range(4):
            greet(device(l, h, part_y, 2 * y + block, d))

    root = jnp.sqrt(weight_ref[...])
    own[...] = (snap_ref[...].astype(jnp.float32) * root[None, :]).astype(jnp.bfloat16)
    pl.semaphore_wait(barrier, 16)

    def remote(src, dst, send, recv, target):
        return pltpu.make_async_remote_copy(
            src_ref=src, dst_ref=dst, send_sem=send, recv_sem=recv, device_id=target, device_id_type=MESH
        )

    def sub_at(piece, sub):
        return rows.at[piece, pl.ds((sub // 4) * PART, PART), pl.ds((sub % 4) * CELL, CELL)]

    def block_at(which, cell_y):
        return cols.at[pl.ds(which * SNAP, SNAP), pl.ds(pl.multiple_of(cell_y * CELL, CELL), CELL)]

    half = lax.rem(z, 2)
    ring_y = z // 2
    a_index = half * 4 + y
    same_ring = (h == l) & (y == ring_y)

    def a_parts(p):
        src = own.at[pl.ds(p * PART, PART), :]
        dst = rows.at[
            p, pl.ds(pl.multiple_of(half * PART, PART), PART), pl.ds(pl.multiple_of(y * CELL, CELL), CELL)
        ]
        return src, dst

    def a_copy(p):
        src, dst = a_parts(p)
        return remote(src, dst, a_send.at[p], a_recv.at[a_index], device(l, h, ring_y, p, d))

    for p in range(8):
        to_self = same_ring & (z == p)

        @pl.when(to_self)
        def _():
            src, dst = a_parts(p)
            pltpu.make_async_copy(src, dst, a_recv.at[a_index]).start()

        @pl.when(jnp.logical_not(to_self))
        def _():
            a_copy(p).start()

    def x_copy(to):
        return remote(own, block_at(l, y), x_send.at[to], x_recv.at[l], device(to, h, y, z, d))

    for to in range(2):
        to_self = (h == to) & (l == h)

        @pl.when(to_self)
        def _():
            pltpu.make_async_copy(own, block_at(l, y), x_recv.at[l]).start()

        @pl.when(jnp.logical_not(to_self))
        def _():
            x_copy(to).start()

    def y_copy(way, which):
        return remote(
            block_at(which, y), block_at(which, y), y_send.at[way, which], y_recv.at[way, which],
            (up_y, down_y)[way],
        )

    def y_arrival(way, which):
        at = block_at(which, turn(y, (-1, 1)[way], 4))
        return remote(at, at, y_send.at[way, which], y_recv.at[way, which], (up_y, down_y)[way])

    def forward_copy(way):
        at = block_at(way, turn(y, (-1, 1)[way], 4))
        return remote(at, at, f_send.at[way], f_recv.at[way], (up_y, down_y)[way])

    def forward_arrival(way):
        at = block_at(way, turn(y, 2, 4))
        return remote(at, at, f_send.at[way], f_recv.at[way], (up_y, down_y)[way])

    def z_copy(way, hop, sub):
        at = sub_at(turn(z, (-hop, hop)[way], 8), sub)
        return remote(at, at, z_send.at[way, hop, sub], z_recv.at[way, hop, sub], (up_z, down_z)[way])

    def z_arrival(way, hop, sub):
        at = sub_at(turn(z, (-hop, hop)[way], 8), sub)
        return remote(at, at, z_send.at[way, hop - 1, sub], z_recv.at[way, hop - 1, sub], (up_z, down_z)[way])

    def x_wait(which):
        at = block_at(which, y)
        remote(at, at, x_send.at[0], x_recv.at[which], partner).wait_recv()
        for way in range(2):
            y_copy(way, which).start()

    for sub in range(8):
        at = sub_at(z, sub)
        remote(at, at, a_send.at[0], a_recv.at[sub], partner).wait_recv()
        for way in range(2):
            z_copy(way, 0, sub).start()
        if sub == 3:
            x_wait(0)
    x_wait(1)

    for hop in range(1, 4):
        for sub in range(8):
            for way in range(2):
                z_arrival(way, hop, sub).wait_recv()
                if hop < 3 or sub // 4 == way:
                    z_copy(way, hop, sub).start()
        if hop == 1:
            for way in range(2):
                y_arrival(way, way).wait_recv()
                forward_copy(way).start()
    for way in range(2):
        y_arrival(way, 1 - way).wait_recv()
        forward_arrival(way).wait_recv()

    def piece_of(step):
        behind = lax.rem(step, 2)
        off = (step + 1) // 2
        return lax.rem(z + 8 + jnp.where(behind == 1, -off, off), 8)

    def peer_copy(step):
        return remote(partial.at[step, 1 - d], peer.at[step], p_send.at[step], p_recv.at[step], sibling)

    def half_copy(step):
        return remote(half_out.at[step], half_in.at[step], q_send.at[step], q_recv.at[step], partner)

    def multiply(step):
        left = rows[piece_of(step)]
        for which in range(2):
            for side in range(2):
                right = cols[pl.ds(which * SNAP + side * COLS, COLS), :]
                partial[step, side, which] = lax.dot_general(
                    left, right, (((1,), (1,)), ((), ())), preferred_element_type=jnp.float32
                )
        peer_copy(step).start()

    def sum_cores(step):
        peer_copy(step).wait_recv()
        half_out[step] = (partial[step, d, 1 - l] + peer[step, 1 - l]).astype(jnp.bfloat16)
        half_copy(step).start()

    def sum_chips(step):
        half_copy(step).wait_recv()
        total = partial[step, d, l] + peer[step, l] + half_in[step].astype(jnp.float32)
        total = total * jnp.float32(1.0 / CELLS)
        at = pl.multiple_of(piece_of(step) * PART, PART)
        out_ref[pl.ds(at, PART), :] = total[:PART]
        out_ref[pl.ds(SNAP + at, PART), :] = total[PART:]

    @pl.loop(0, 10)
    def _(step):
        @pl.when(step == 7)
        def _():
            for sub in range(8):
                z_arrival(sub // 4, 4, sub).wait_recv()

        @pl.when(step < 8)
        def _():
            multiply(step)

        @pl.when((step >= 1) & (step < 9))
        def _():
            sum_cores(step - 1)

        @pl.when(step >= 2)
        def _():
            sum_chips(step - 2)

    for p in range(8):

        @pl.when(jnp.logical_not(same_ring & (z == p)))
        def _():
            a_copy(p).wait_send()

    for to in range(2):

        @pl.when(jnp.logical_not((h == to) & (l == h)))
        def _():
            x_copy(to).wait_send()

    for way in range(2):
        for which in range(2):
            y_copy(way, which).wait_send()
        forward_copy(way).wait_send()
        for hop in range(4):
            for sub in range(8):
                if hop < 3 or sub // 4 == way:
                    z_copy(way, hop, sub).wait_send()
    for step in range(8):
        peer_copy(step).wait_send()
        half_copy(step).wait_send()


def on_device(snapshots, cell_weight):
    vmem = pl.BlockSpec(memory_space=pltpu.VMEM)
    dma = pltpu.SemaphoreType.DMA
    return pl.pallas_call(
        kernel,
        out_shape=jax.ShapeDtypeStruct((2 * SNAP, COLS), jnp.float32),
        in_specs=[vmem, vmem],
        out_specs=vmem,
        scratch_shapes=[
            pltpu.VMEM((SNAP, CELL), jnp.bfloat16),
            pltpu.VMEM((2 * SNAP, 4 * CELL), jnp.bfloat16),
            pltpu.VMEM((8, 2 * PART, 4 * CELL), jnp.bfloat16),
            pltpu.VMEM((8, 2, 2, 2 * PART, COLS), jnp.float32),
            pltpu.VMEM((8, 2, 2 * PART, COLS), jnp.float32),
            pltpu.VMEM((8, 2 * PART, COLS), jnp.bfloat16),
            pltpu.VMEM((8, 2 * PART, COLS), jnp.bfloat16),
            dma((8,)), dma((8,)), dma((2,)), dma((2,)), dma((2, 2)), dma((2, 2)), dma((2,)), dma((2,)),
            dma((2, 4, 8)), dma((2, 4, 8)), dma((8,)), dma((8,)), dma((8,)), dma((8,)),
        ],
        compiler_params=pltpu.CompilerParams(
            collective_id=0, has_side_effects=True, vmem_limit_bytes=48 << 20
        ),
        name="gram",
    )(snapshots, cell_weight)


def solution(mesh):
    return jax.shard_map(
        on_device,
        mesh=mesh,
        in_specs=(P("col", ("row", "depth")), P(("row", "depth"))),
        out_specs=P("row", ("col", "depth")),
        check_vma=False,
    )
```

```python
import jax
import jax.numpy as jnp
from jax import lax
from jax.experimental import pallas as pl
from jax.experimental.pallas import tpu as pltpu
from jax.sharding import PartitionSpec as P

MESH = pl.DeviceIdType.MESH
CELLS = 6144
SNAP = 512
CELL = 384
PART = 64
PIECE = 2 * PART
COLS = 256
CHUNK = 128
CHUNKS = SNAP // CHUNK

OWN, OPPOSITE, HOP1, HOP2, HOP3 = (0, 1), (1, 1), (2, 2), (4, 2), (6, 2)
GROUPS = (OWN, HOP1, HOP2, HOP3, OPPOSITE)


def kernel(
    snap_ref, weight_ref, out_ref, raw, weight, own, relay, cols, rows, partial, peer, half_out, half_in,
    in_sem, a_send, a_recv, r_recv, x_send, x_recv, y_send, y_recv, f_send, f_recv,
    z_send, z_recv, p_send, p_recv, q_send, q_recv,
):
    row, col, d = lax.axis_index("row"), lax.axis_index("col"), lax.axis_index("depth")
    h, y, l, z = row // 4, lax.rem(row, 4), col // 8, lax.rem(col, 8)

    def device(h, l, y, z, d):
        return (h * 4 + y, l * 8 + z, d)

    def turn(value, by, size):
        return lax.rem(value + by + size, size)

    along_y = [device(h, l, turn(y, by, 4), z, d) for by in (1, -1)]
    along_z = [device(h, l, y, turn(z, by, 8), d) for by in (1, -1)]
    sibling = device(h, l, y, z, 1 - d)
    partner = device(h, 1 - l, y, z, d)
    opposite = device(1 - h, 1 - l, y, z, d)
    outer = h == l
    inner = h != l

    load = [
        pltpu.make_async_copy(snap_ref, raw, in_sem.at[0]),
        pltpu.make_async_copy(weight_ref, weight, in_sem.at[1]),
    ]
    for copy in load:
        copy.start()

    barrier = pltpu.get_barrier_semaphore()

    def greet(target):
        pl.semaphore_signal(barrier, inc=1, device_id=target, device_id_type=MESH)

    for target in (opposite, partner, sibling, *along_y, *along_z):
        greet(target)
    for block in range(2):
        for part_y in range(4):
            greet(device(h, l, part_y, 2 * y + block, d))

    for copy in load:
        copy.wait()
    root = jnp.sqrt(weight[...])
    own[...] = (raw[...].astype(jnp.float32) * root[None, :]).astype(jnp.bfloat16)

    @pl.when(outer)
    def _():
        at = pl.ds(pl.multiple_of(l * SNAP, SNAP), SNAP), pl.ds(pl.multiple_of(y * CELL, CELL), CELL)
        cols[at] = own[...]

    pl.semaphore_wait(barrier, 15)

    def remote(src, dst, send, recv, target):
        return pltpu.make_async_remote_copy(
            src_ref=src, dst_ref=dst, send_sem=send, recv_sem=recv, device_id=target, device_id_type=MESH
        )

    def sub_at(slot, sub):
        return rows.at[pl.ds(slot * PIECE + (sub // 4) * PART, PART), pl.ds((sub % 4) * CELL, CELL)]

    def chunk_at(which, chunk, cell_y):
        at = pl.multiple_of(which * SNAP + chunk * CHUNK, CHUNK)
        return cols.at[pl.ds(at, CHUNK), pl.ds(pl.multiple_of(cell_y * CELL, CELL), CELL)]

    def x_opposite(chunk, to_relay):
        src = own.at[pl.ds(chunk * CHUNK, CHUNK), :]
        if to_relay:
            return remote(src, relay.at[pl.ds(chunk * CHUNK, CHUNK), :], x_send.at[0, chunk], r_recv.at[chunk], opposite)
        return remote(src, chunk_at(l, chunk, y), x_send.at[0, chunk], x_recv.at[0, chunk], opposite)

    def x_partner(chunk, from_relay):
        if from_relay:
            src, which, first = relay.at[pl.ds(chunk * CHUNK, CHUNK), :], 1 - l, 1
        else:
            src, which, first = own.at[pl.ds(chunk * CHUNK, CHUNK), :], l, 0
        return remote(src, chunk_at(which, chunk, y), x_send.at[1, chunk], x_recv.at[first, chunk], partner)

    def x_start(chunk):
        @pl.when(outer)
        def _():
            x_opposite(chunk, True).start()

        @pl.when(inner)
        def _():
            x_opposite(chunk, False).start()
            x_partner(chunk, False).start()

    def x_relay(chunk):
        @pl.when(outer)
        def _():
            x_opposite(chunk, True).wait_recv()
            x_partner(chunk, True).start()

    half = lax.rem(z, 2)
    ring_y = z // 2
    a_index = half * 4 + y

    def a_copy(p, to_self):
        lanes = pl.ds(pl.multiple_of(y * CELL, CELL), CELL)
        src = cols.at[pl.ds(pl.multiple_of(h * SNAP + p * PART, PART), PART), lanes]
        dst = rows.at[pl.ds(pl.multiple_of(half * PART, PART), PART), lanes]
        if to_self:
            return pltpu.make_async_copy(src, dst, a_recv.at[a_index])
        return remote(src, dst, a_send.at[p], a_recv.at[a_index], device(h, l, ring_y, p, d))

    def a_start(chunk):
        for p in range(chunk * CHUNK // PART, (chunk + 1) * CHUNK // PART):

            @pl.when((y == ring_y) & (z == p))
            def _():
                a_copy(p, True).start()

            @pl.when((y != ring_y) | (z != p))
            def _():
                a_copy(p, False).start()

    def block_of(turn_of):
        return 1 - l if turn_of == 0 else l

    def y_copy(way, first, chunk):
        at = chunk_at(block_of(first), chunk, y)
        return remote(at, at, y_send.at[way, first, chunk], y_recv.at[way, first, chunk], along_y[way])

    def y_arrival(way, first, chunk):
        at = chunk_at(block_of(first), chunk, turn(y, (-1, 1)[way], 4))
        return remote(at, at, y_send.at[way, first, chunk], y_recv.at[way, first, chunk], along_y[way])

    def way_of(chunk):
        return chunk % 2

    def forward(first, chunk):
        way = way_of(chunk)
        y_arrival(way, first, chunk).wait_recv()
        forward_copy(first, chunk).start()

    def forward_copy(first, chunk):
        way = way_of(chunk)
        at = chunk_at(block_of(first), chunk, turn(y, (-1, 1)[way], 4))
        return remote(at, at, f_send.at[first, chunk], f_recv.at[first, chunk], along_y[way])

    def forward_arrival(first, chunk):
        at = chunk_at(block_of(first), chunk, turn(y, 2, 4))
        return remote(at, at, f_send.at[first, chunk], f_recv.at[first, chunk], along_y[way_of(chunk)])

    def x_wait(first, chunk):
        at = chunk_at(block_of(first), chunk, y)
        remote(at, at, x_send.at[0, chunk], x_recv.at[first, chunk], partner).wait_recv()

    def y_start(first, chunk):
        for way in (way_of(chunk), 1 - way_of(chunk)):
            y_copy(way, first, chunk).start()

    def y_finish(first):
        for chunk in range(CHUNKS):
            y_arrival(1 - way_of(chunk), first, chunk).wait_recv()
            forward_arrival(first, chunk).wait_recv()

    def slot_of(way, hop):
        return {0: 0, 4: 1}.get(hop, 2 * hop + way)

    def z_copy(way, hop, sub):
        return remote(
            sub_at(slot_of(way, hop), sub), sub_at(slot_of(way, hop + 1), sub),
            z_send.at[way, hop, sub], z_recv.at[way, hop, sub], along_z[way],
        )

    def z_wait(way, hop, sub):
        at = sub_at(slot_of(way, hop), sub)
        remote(at, at, z_send.at[way, hop - 1, sub], z_recv.at[way, hop - 1, sub], along_z[way]).wait_recv()

    def z_step(hop, sub):
        for way in range(2):
            z_wait(way, hop, sub)
            if hop < 3 or sub // 4 == way:
                z_copy(way, hop, sub).start()

    def rows_of(group):
        return pl.ds(group[0] * PIECE, group[1] * PIECE)

    def peer_copy(group, first):
        which, g = block_of(first), GROUPS.index(group)
        return remote(
            partial.at[1 - d, which, rows_of(group)], peer.at[which, rows_of(group)],
            p_send.at[first, g], p_recv.at[first, g], sibling,
        )

    def half_copy(group):
        g = GROUPS.index(group)
        return remote(
            half_out.at[rows_of(group)], half_in.at[rows_of(group)], q_send.at[g], q_recv.at[g], partner
        )

    def multiply(group, first):
        left = rows[rows_of(group), :]
        which = block_of(first)
        for side in range(2):
            at = pl.multiple_of(which * SNAP + side * COLS, COLS)
            partial[side, which, rows_of(group)] = lax.dot_general(
                left, cols[pl.ds(at, COLS), :], (((1,), (1,)), ((), ())), preferred_element_type=jnp.float32
            )
        peer_copy(group, first).start()

    def sum_cores(group):
        peer_copy(group, 0).wait_recv()
        at = rows_of(group)
        half_out[at] = (partial[d, 1 - l, at] + peer[1 - l, at]).astype(jnp.bfloat16)
        half_copy(group).start()

    def sum_chips(group):
        peer_copy(group, 1).wait_recv()
        half_copy(group).wait_recv()
        at = rows_of(group)
        total = partial[d, l, at] + peer[l, at] + half_in[at].astype(jnp.float32)
        total = total * jnp.float32(1.0 / CELLS)
        for i in range(group[1]):
            off = {OWN: 0, OPPOSITE: 4}.get(group, (-1, 1)[i] * (group[0] // 2))
            to = pl.multiple_of(turn(z, off, 8) * PART, PART)
            out_ref[pl.ds(to, PART), :] = total[i * PIECE : i * PIECE + PART]
            out_ref[pl.ds(SNAP + to, PART), :] = total[i * PIECE + PART : (i + 1) * PIECE]

    def z_first(sub):
        at = sub_at(0, sub)
        remote(at, at, a_send.at[0], a_recv.at[sub], partner).wait_recv()
        for way in range(2):
            z_copy(way, 0, sub).start()

    for i in range(CHUNKS):
        x_start(i)

        @pl.when(outer)
        def _():
            a_start(i)

    for i in range(CHUNKS):
        x_relay(i)
        x_wait(0, i)

        @pl.when(inner)
        def _():
            a_start(i)

        y_start(0, i)
    for i in range(CHUNKS):

        @pl.when(inner)
        def _():
            x_wait(1, i)

        y_start(1, i)
        forward(0, i)
        z_first(2 * i)
        z_first(2 * i + 1)
    for sub in range(8):
        z_step(1, sub)
        if sub >= 6:
            forward(1, sub - 6)
    y_finish(0)
    multiply(OWN, 0)
    multiply(HOP1, 0)
    for sub in range(8):
        z_step(2, sub)
        if sub in (1, 3):
            forward(1, 2 + sub // 2)
        if sub == 3:
            sum_cores(OWN)
            sum_cores(HOP1)
    multiply(HOP2, 0)
    for sub in range(8):
        z_step(3, sub)
        if sub == 3:
            sum_cores(HOP2)
    multiply(HOP3, 0)
    y_finish(1)
    multiply(OWN, 1)
    multiply(HOP1, 1)
    sum_cores(HOP3)
    multiply(HOP2, 1)
    sum_chips(OWN)
    multiply(HOP3, 1)
    for sub in range(8):
        z_wait(sub // 4, 4, sub)
    multiply(OPPOSITE, 0)
    multiply(OPPOSITE, 1)
    sum_cores(OPPOSITE)
    sum_chips(HOP1)
    sum_chips(HOP2)
    sum_chips(HOP3)
    sum_chips(OPPOSITE)

    for p in range(8):

        @pl.when((y != ring_y) | (z != p))
        def _():
            a_copy(p, False).wait_send()

    for chunk in range(CHUNKS):
        x_opposite(chunk, True).wait_send()
        x_partner(chunk, True).wait_send()
    for first in range(2):
        for chunk in range(CHUNKS):
            for way in range(2):
                y_copy(way, first, chunk).wait_send()
            forward_copy(first, chunk).wait_send()
    for way in range(2):
        for hop in range(4):
            for sub in range(8):
                if hop < 3 or sub // 4 == way:
                    z_copy(way, hop, sub).wait_send()
    for group in GROUPS:
        for first in range(2):
            peer_copy(group, first).wait_send()
        half_copy(group).wait_send()


def on_device(snapshots, cell_weight):
    hbm = pl.BlockSpec(memory_space=pltpu.HBM)
    dma = pltpu.SemaphoreType.DMA
    return pl.pallas_call(
        kernel,
        out_shape=jax.ShapeDtypeStruct((2 * SNAP, COLS), jnp.float32),
        in_specs=[hbm, hbm],
        out_specs=pl.BlockSpec(memory_space=pltpu.VMEM),
        scratch_shapes=[
            pltpu.VMEM((SNAP, CELL), jnp.bfloat16),
            pltpu.VMEM((CELL,), jnp.float32),
            pltpu.VMEM((SNAP, CELL), jnp.bfloat16),
            pltpu.VMEM((SNAP, CELL), jnp.bfloat16),
            pltpu.VMEM((2 * SNAP, 4 * CELL), jnp.bfloat16),
            pltpu.VMEM((8 * PIECE, 4 * CELL), jnp.bfloat16),
            pltpu.VMEM((2, 2, 8 * PIECE, COLS), jnp.float32),
            pltpu.VMEM((2, 8 * PIECE, COLS), jnp.float32),
            pltpu.VMEM((8 * PIECE, COLS), jnp.bfloat16),
            pltpu.VMEM((8 * PIECE, COLS), jnp.bfloat16),
            dma((2,)),
            dma((8,)), dma((8,)),
            dma((CHUNKS,)), dma((2, CHUNKS)), dma((2, CHUNKS)),
            dma((2, 2, CHUNKS)), dma((2, 2, CHUNKS)),
            dma((2, CHUNKS)), dma((2, CHUNKS)),
            dma((2, 4, 8)), dma((2, 4, 8)),
            dma((2, 5)), dma((2, 5)), dma((5,)), dma((5,)),
        ],
        compiler_params=pltpu.CompilerParams(
            collective_id=0, has_side_effects=True, vmem_limit_bytes=60 << 20
        ),
        name="gram",
    )(snapshots, cell_weight)


def solution(mesh):
    return jax.shard_map(
        on_device,
        mesh=mesh,
        in_specs=(P("col", ("row", "depth")), P(("row", "depth"))),
        out_specs=P("row", ("col", "depth")),
        check_vma=False,
    )
```

```python
import jax
import jax.numpy as jnp
from jax import lax
from jax.experimental import pallas as pl
from jax.experimental.pallas import tpu as pltpu
from jax.sharding import PartitionSpec as P

MESH = pl.DeviceIdType.MESH
CELLS = 6144
SNAP = 512
CELL = 384
PART = 64
PIECE = 2 * PART
COLS = 256
CHUNK = 128
CHUNKS = SNAP // CHUNK

OWN, OPPOSITE, HOP1, HOP2, HOP3 = (0, 1), (1, 1), (2, 2), (4, 2), (6, 2)
GROUPS = (OWN, HOP1, HOP2, HOP3, OPPOSITE)


def kernel(
    snap_ref, weight_ref, out_ref, raw, weight, own, relay, cols, rows, partial, peer, half_out, half_in,
    in_sem, a_send, a_recv, r_recv, x_send, x_recv, y_send, y_recv, f_send, f_recv,
    z_send, z_recv, p_send, p_recv, q_send, q_recv,
):
    row, col, d = lax.axis_index("row"), lax.axis_index("col"), lax.axis_index("depth")
    h, y, l, z = row // 4, lax.rem(row, 4), col // 8, lax.rem(col, 8)

    def device(h, l, y, z, d):
        return (h * 4 + y, l * 8 + z, d)

    def turn(value, by, size):
        return lax.rem(value + by + size, size)

    along_y = [device(h, l, turn(y, by, 4), z, d) for by in (1, -1)]
    along_z = [device(h, l, y, turn(z, by, 8), d) for by in (1, -1)]
    sibling = device(h, l, y, z, 1 - d)
    partner = device(h, 1 - l, y, z, d)
    opposite = device(1 - h, 1 - l, y, z, d)
    outer = h == l
    inner = h != l

    load = [
        pltpu.make_async_copy(snap_ref, raw, in_sem.at[0]),
        pltpu.make_async_copy(weight_ref, weight, in_sem.at[1]),
    ]
    for copy in load:
        copy.start()

    barrier = pltpu.get_barrier_semaphore()

    def greet(target):
        pl.semaphore_signal(barrier, inc=1, device_id=target, device_id_type=MESH)

    for target in (opposite, partner, sibling, *along_y, *along_z):
        greet(target)
    for block in range(2):
        for part_y in range(4):
            greet(device(l, h, part_y, 2 * y + block, d))

    for copy in load:
        copy.wait()
    root = jnp.sqrt(weight[...])
    own[...] = (raw[...].astype(jnp.float32) * root[None, :]).astype(jnp.bfloat16)

    @pl.when(outer)
    def _():
        at = pl.ds(pl.multiple_of(l * SNAP, SNAP), SNAP), pl.ds(pl.multiple_of(y * CELL, CELL), CELL)
        cols[at] = own[...]

    pl.semaphore_wait(barrier, 15)

    def remote(src, dst, send, recv, target):
        return pltpu.make_async_remote_copy(
            src_ref=src, dst_ref=dst, send_sem=send, recv_sem=recv, device_id=target, device_id_type=MESH
        )

    def sub_at(slot, sub):
        return rows.at[pl.ds(slot * PIECE + (sub // 4) * PART, PART), pl.ds((sub % 4) * CELL, CELL)]

    def chunk_at(which, chunk, cell_y):
        at = pl.multiple_of(which * SNAP + chunk * CHUNK, CHUNK)
        return cols.at[pl.ds(at, CHUNK), pl.ds(pl.multiple_of(cell_y * CELL, CELL), CELL)]

    def x_opposite(chunk, to_relay):
        src = own.at[pl.ds(chunk * CHUNK, CHUNK), :]
        if to_relay:
            return remote(src, relay.at[pl.ds(chunk * CHUNK, CHUNK), :], x_send.at[0, chunk], r_recv.at[chunk], opposite)
        return remote(src, chunk_at(l, chunk, y), x_send.at[0, chunk], x_recv.at[0, chunk], opposite)

    def x_partner(chunk, from_relay):
        if from_relay:
            src, which, first = relay.at[pl.ds(chunk * CHUNK, CHUNK), :], 1 - l, 1
        else:
            src, which, first = own.at[pl.ds(chunk * CHUNK, CHUNK), :], l, 0
        return remote(src, chunk_at(which, chunk, y), x_send.at[1, chunk], x_recv.at[first, chunk], partner)

    def x_start(chunk):
        @pl.when(outer)
        def _():
            x_opposite(chunk, True).start()

        @pl.when(inner)
        def _():
            x_opposite(chunk, False).start()
            x_partner(chunk, False).start()

    def x_relay(chunk):
        @pl.when(outer)
        def _():
            x_opposite(chunk, True).wait_recv()
            x_partner(chunk, True).start()

    half = lax.rem(z, 2)
    ring_y = z // 2
    a_index = half * 4 + y

    def stays(p):
        return outer & (y == ring_y) & (z == p)

    def a_copy(p, to_self):
        src = own.at[pl.ds(p * PART, PART), :]
        dst = rows.at[pl.ds(pl.multiple_of(half * PART, PART), PART), pl.ds(pl.multiple_of(y * CELL, CELL), CELL)]
        if to_self:
            return pltpu.make_async_copy(src, dst, a_recv.at[a_index])
        return remote(src, dst, a_send.at[p], a_recv.at[a_index], device(l, h, ring_y, p, d))

    def a_start(p):
        @pl.when(stays(p))
        def _():
            a_copy(p, True).start()

        @pl.when(jnp.logical_not(stays(p)))
        def _():
            a_copy(p, False).start()

    def block_of(turn_of):
        return 1 - l if turn_of == 0 else l

    def y_copy(way, first, chunk):
        at = chunk_at(block_of(first), chunk, y)
        return remote(at, at, y_send.at[way, first, chunk], y_recv.at[way, first, chunk], along_y[way])

    def y_arrival(way, first, chunk):
        at = chunk_at(block_of(first), chunk, turn(y, (-1, 1)[way], 4))
        return remote(at, at, y_send.at[way, first, chunk], y_recv.at[way, first, chunk], along_y[way])

    def way_of(chunk):
        return chunk % 2

    def forward(first, chunk):
        way = way_of(chunk)
        y_arrival(way, first, chunk).wait_recv()
        forward_copy(first, chunk).start()

    def forward_copy(first, chunk):
        way = way_of(chunk)
        at = chunk_at(block_of(first), chunk, turn(y, (-1, 1)[way], 4))
        return remote(at, at, f_send.at[first, chunk], f_recv.at[first, chunk], along_y[way])

    def forward_arrival(first, chunk):
        at = chunk_at(block_of(first), chunk, turn(y, 2, 4))
        return remote(at, at, f_send.at[first, chunk], f_recv.at[first, chunk], along_y[way_of(chunk)])

    def x_wait(first, chunk):
        at = chunk_at(block_of(first), chunk, y)
        remote(at, at, x_send.at[0, chunk], x_recv.at[first, chunk], partner).wait_recv()

    def y_start(first, chunk):
        for way in (way_of(chunk), 1 - way_of(chunk)):
            y_copy(way, first, chunk).start()

    def y_finish(first):
        for chunk in range(CHUNKS):
            y_arrival(1 - way_of(chunk), first, chunk).wait_recv()
            forward_arrival(first, chunk).wait_recv()

    def slot_of(way, hop):
        return {0: 0, 4: 1}.get(hop, 2 * hop + way)

    def z_copy(way, hop, sub):
        return remote(
            sub_at(slot_of(way, hop), sub), sub_at(slot_of(way, hop + 1), sub),
            z_send.at[way, hop, sub], z_recv.at[way, hop, sub], along_z[way],
        )

    def z_wait(way, hop, sub):
        at = sub_at(slot_of(way, hop), sub)
        remote(at, at, z_send.at[way, hop - 1, sub], z_recv.at[way, hop - 1, sub], along_z[way]).wait_recv()

    def z_step(hop, sub):
        for way in range(2):
            z_wait(way, hop, sub)
            if hop < 3 or sub // 4 == way:
                z_copy(way, hop, sub).start()

    def rows_of(group):
        return pl.ds(group[0] * PIECE, group[1] * PIECE)

    def peer_copy(group, first):
        which, g = block_of(first), GROUPS.index(group)
        return remote(
            partial.at[1 - d, which, rows_of(group)], peer.at[which, rows_of(group)],
            p_send.at[first, g], p_recv.at[first, g], sibling,
        )

    def half_copy(group):
        g = GROUPS.index(group)
        return remote(
            half_out.at[rows_of(group)], half_in.at[rows_of(group)], q_send.at[g], q_recv.at[g], partner
        )

    def multiply(group, first):
        left = rows[rows_of(group), :]
        which = block_of(first)
        for side in range(2):
            at = pl.multiple_of(which * SNAP + side * COLS, COLS)
            partial[side, which, rows_of(group)] = lax.dot_general(
                left, cols[pl.ds(at, COLS), :], (((1,), (1,)), ((), ())), preferred_element_type=jnp.float32
            )
        peer_copy(group, first).start()

    def sum_cores(group):
        peer_copy(group, 0).wait_recv()
        at = rows_of(group)
        half_out[at] = (partial[d, 1 - l, at] + peer[1 - l, at]).astype(jnp.bfloat16)
        half_copy(group).start()

    def sum_chips(group):
        peer_copy(group, 1).wait_recv()
        half_copy(group).wait_recv()
        at = rows_of(group)
        total = partial[d, l, at] + peer[l, at] + half_in[at].astype(jnp.float32)
        total = total * jnp.float32(1.0 / CELLS)
        for i in range(group[1]):
            off = {OWN: 0, OPPOSITE: 4}.get(group, (-1, 1)[i] * (group[0] // 2))
            to = pl.multiple_of(turn(z, off, 8) * PART, PART)
            out_ref[pl.ds(to, PART), :] = total[i * PIECE : i * PIECE + PART]
            out_ref[pl.ds(SNAP + to, PART), :] = total[i * PIECE + PART : (i + 1) * PIECE]

    def z_first(sub):
        at = sub_at(0, sub)
        remote(at, at, a_send.at[0], a_recv.at[sub], partner).wait_recv()
        for way in range(2):
            z_copy(way, 0, sub).start()

    def y_second(chunk):
        @pl.when(inner)
        def _():
            x_wait(1, chunk)

        y_start(1, chunk)

    def y_first(chunk):
        x_wait(0, chunk)
        y_start(0, chunk)

    for p in range(8):
        a_start(p)
    for i in range(CHUNKS):
        x_start(i)
    for i in range(CHUNKS):
        x_relay(i)
        if i >= 2:
            y_second(i - 2)
    for sub in range(8):
        z_first(sub)
    for sub in range(8):
        z_step(1, sub)
        if sub % 2 == 1:
            y_first(sub // 2)
    for sub in range(8):
        z_step(2, sub)
        if sub in (0, 1, 2, 4):
            forward(0, (0, 1, 2, None, 3)[sub])
        if sub == 1:
            y_second(2)
            y_second(3)
    y_finish(0)
    multiply(OWN, 0)
    multiply(HOP1, 0)
    for sub in range(8):
        z_step(3, sub)
        if sub < 4:
            forward(1, sub)
        if sub == 3:
            sum_cores(OWN)
            sum_cores(HOP1)
    multiply(HOP2, 0)
    sum_cores(HOP2)
    multiply(HOP3, 0)
    y_finish(1)
    multiply(OWN, 1)
    multiply(HOP1, 1)
    sum_cores(HOP3)
    multiply(HOP2, 1)
    sum_chips(OWN)
    multiply(HOP3, 1)
    for sub in range(8):
        z_wait(sub // 4, 4, sub)
    multiply(OPPOSITE, 0)
    multiply(OPPOSITE, 1)
    sum_cores(OPPOSITE)
    sum_chips(HOP1)
    sum_chips(HOP2)
    sum_chips(HOP3)
    sum_chips(OPPOSITE)

    for p in range(8):

        @pl.when(jnp.logical_not(stays(p)))
        def _():
            a_copy(p, False).wait_send()

    for chunk in range(CHUNKS):
        x_opposite(chunk, True).wait_send()
        x_partner(chunk, True).wait_send()
    for first in range(2):
        for chunk in range(CHUNKS):
            for way in range(2):
                y_copy(way, first, chunk).wait_send()
            forward_copy(first, chunk).wait_send()
    for way in range(2):
        for hop in range(4):
            for sub in range(8):
                if hop < 3 or sub // 4 == way:
                    z_copy(way, hop, sub).wait_send()
    for group in GROUPS:
        for first in range(2):
            peer_copy(group, first).wait_send()
        half_copy(group).wait_send()


def on_device(snapshots, cell_weight):
    hbm = pl.BlockSpec(memory_space=pltpu.HBM)
    dma = pltpu.SemaphoreType.DMA
    return pl.pallas_call(
        kernel,
        out_shape=jax.ShapeDtypeStruct((2 * SNAP, COLS), jnp.float32),
        in_specs=[hbm, hbm],
        out_specs=pl.BlockSpec(memory_space=pltpu.VMEM),
        scratch_shapes=[
            pltpu.VMEM((SNAP, CELL), jnp.bfloat16),
            pltpu.VMEM((CELL,), jnp.float32),
            pltpu.VMEM((SNAP, CELL), jnp.bfloat16),
            pltpu.VMEM((SNAP, CELL), jnp.bfloat16),
            pltpu.VMEM((2 * SNAP, 4 * CELL), jnp.bfloat16),
            pltpu.VMEM((8 * PIECE, 4 * CELL), jnp.bfloat16),
            pltpu.VMEM((2, 2, 8 * PIECE, COLS), jnp.float32),
            pltpu.VMEM((2, 8 * PIECE, COLS), jnp.float32),
            pltpu.VMEM((8 * PIECE, COLS), jnp.bfloat16),
            pltpu.VMEM((8 * PIECE, COLS), jnp.bfloat16),
            dma((2,)),
            dma((8,)), dma((8,)),
            dma((CHUNKS,)), dma((2, CHUNKS)), dma((2, CHUNKS)),
            dma((2, 2, CHUNKS)), dma((2, 2, CHUNKS)),
            dma((2, CHUNKS)), dma((2, CHUNKS)),
            dma((2, 4, 8)), dma((2, 4, 8)),
            dma((2, 5)), dma((2, 5)), dma((5,)), dma((5,)),
        ],
        compiler_params=pltpu.CompilerParams(
            collective_id=0, has_side_effects=True, vmem_limit_bytes=40 << 20
        ),
        name="gram",
    )(pltpu.with_memory_space_constraint(snapshots, pltpu.HBM), pltpu.with_memory_space_constraint(cell_weight, pltpu.HBM))


def solution(mesh):
    return jax.shard_map(
        on_device,
        mesh=mesh,
        in_specs=(P("col", ("row", "depth")), P(("row", "depth"))),
        out_specs=P("row", ("col", "depth")),
        check_vma=False,
    )
```

```python
import jax
import jax.numpy as jnp
from jax import lax
from jax.experimental import pallas as pl
from jax.experimental.pallas import tpu as pltpu
from jax.sharding import PartitionSpec as P

MESH = pl.DeviceIdType.MESH
CELLS = 6144
SNAP = 512
CELL = 384
PART = 64
PIECE = 2 * PART
COLS = 256
CHUNK = 128
CHUNKS = SNAP // CHUNK
STRIP = 16

OWN, HOP1, HOP2, HOP3 = (0, PIECE), (2 * PIECE, 2 * PIECE), (4 * PIECE, 2 * PIECE), (6 * PIECE, 2 * PIECE)
LAST = (PIECE, PIECE)
GROUPS = (OWN, HOP1, HOP2, HOP3, LAST)


def kernel(
    snap_ref, weight_ref, out_ref, raw, weight, own, relay, cols, rows, partial, peer, half_out, half_in,
    in_sem, a_send, a_recv, r_recv, x_send, x_recv, y_send, y_recv, f_send, f_recv,
    z_send, z_recv, p_send, p_recv, q_send, q_recv,
):
    row, col, d = lax.axis_index("row"), lax.axis_index("col"), lax.axis_index("depth")
    h, y, l, z = row // 4, lax.rem(row, 4), col // 8, lax.rem(col, 8)

    def device(h, l, y, z, d):
        return (h * 4 + y, l * 8 + z, d)

    def turn(value, by, size):
        return lax.rem(value + by + size, size)

    along_y = [device(h, l, turn(y, by, 4), z, d) for by in (1, -1)]
    along_z = [device(h, l, y, turn(z, by, 8), d) for by in (1, -1)]
    sibling = device(h, l, y, z, 1 - d)
    partner = device(h, 1 - l, y, z, d)
    opposite = device(1 - h, 1 - l, y, z, d)
    outer = h == l
    inner = h != l

    load = [
        pltpu.make_async_copy(snap_ref, raw, in_sem.at[0]),
        pltpu.make_async_copy(weight_ref, weight, in_sem.at[1]),
    ]
    for copy in load:
        copy.start()

    barrier = pltpu.get_barrier_semaphore()

    def greet(target):
        pl.semaphore_signal(barrier, inc=1, device_id=target, device_id_type=MESH)

    for target in (opposite, partner, sibling, *along_y, *along_z):
        greet(target)
    for block in range(2):
        for part_y in range(4):
            greet(device(l, h, part_y, 2 * y + block, d))

    for copy in load:
        copy.wait()
    root = jnp.sqrt(weight[...])
    own[...] = (raw[...].astype(jnp.float32) * root[None, :]).astype(jnp.bfloat16)

    @pl.when(outer)
    def _():
        at = pl.ds(pl.multiple_of(l * SNAP, SNAP), SNAP), pl.ds(pl.multiple_of(y * CELL, CELL), CELL)
        cols[at] = own[...]

    pl.semaphore_wait(barrier, 15)

    def remote(src, dst, send, recv, target):
        return pltpu.make_async_remote_copy(
            src_ref=src, dst_ref=dst, send_sem=send, recv_sem=recv, device_id=target, device_id_type=MESH
        )

    def sub_at(slot, sub):
        return rows.at[pl.ds(slot * PIECE + sub * STRIP, STRIP), :]

    def chunk_at(which, chunk, cell_y):
        at = pl.multiple_of(which * SNAP + chunk * CHUNK, CHUNK)
        return cols.at[pl.ds(at, CHUNK), pl.ds(pl.multiple_of(cell_y * CELL, CELL), CELL)]

    def x_opposite(chunk, to_relay):
        src = own.at[pl.ds(chunk * CHUNK, CHUNK), :]
        if to_relay:
            return remote(src, relay.at[pl.ds(chunk * CHUNK, CHUNK), :], x_send.at[0, chunk], r_recv.at[chunk], opposite)
        return remote(src, chunk_at(l, chunk, y), x_send.at[0, chunk], x_recv.at[0, chunk], opposite)

    def x_partner(chunk, from_relay):
        if from_relay:
            src, which, first = relay.at[pl.ds(chunk * CHUNK, CHUNK), :], 1 - l, 1
        else:
            src, which, first = own.at[pl.ds(chunk * CHUNK, CHUNK), :], l, 0
        return remote(src, chunk_at(which, chunk, y), x_send.at[1, chunk], x_recv.at[first, chunk], partner)

    def x_relay(chunk):
        @pl.when(outer)
        def _():
            x_opposite(chunk, True).wait_recv()
            x_partner(chunk, True).start()

    half = lax.rem(z, 2)
    ring_y = z // 2
    a_index = half * 4 + y

    def stays(p):
        return outer & (y == ring_y) & (z == p)

    def a_copy(chunk, p, to_self):
        src = own.at[pl.ds(chunk * CHUNK + p * STRIP, STRIP), :]
        dst = rows.at[
            pl.ds(pl.multiple_of((2 * chunk + half) * STRIP, STRIP), STRIP),
            pl.ds(pl.multiple_of(y * CELL, CELL), CELL),
        ]
        recv = a_recv.at[chunk, a_index]
        if to_self:
            return pltpu.make_async_copy(src, dst, recv)
        return remote(src, dst, a_send.at[chunk, p], recv, device(l, h, ring_y, p, d))

    def a_start(chunk):
        for p in range(8):

            @pl.when(stays(p))
            def _():
                a_copy(chunk, p, True).start()

            @pl.when(jnp.logical_not(stays(p)))
            def _():
                a_copy(chunk, p, False).start()

    def a_wait(chunk, block):
        for cell_y in range(4):
            at = rows.at[pl.ds((2 * chunk + block) * STRIP, STRIP), pl.ds(cell_y * CELL, CELL)]
            remote(at, at, a_send.at[0, 0], a_recv.at[chunk, block * 4 + cell_y], partner).wait_recv()

    def block_of(turn_of):
        return 1 - l if turn_of == 0 else l

    def y_copy(way, first, chunk):
        at = chunk_at(block_of(first), chunk, y)
        return remote(at, at, y_send.at[way, first, chunk], y_recv.at[way, first, chunk], along_y[way])

    def y_arrival(way, first, chunk):
        at = chunk_at(block_of(first), chunk, turn(y, (-1, 1)[way], 4))
        return remote(at, at, y_send.at[way, first, chunk], y_recv.at[way, first, chunk], along_y[way])

    def way_of(chunk):
        return chunk % 2

    def forward(first, chunk):
        way = way_of(chunk)
        y_arrival(way, first, chunk).wait_recv()
        forward_copy(first, chunk).start()

    def forward_copy(first, chunk):
        way = way_of(chunk)
        at = chunk_at(block_of(first), chunk, turn(y, (-1, 1)[way], 4))
        return remote(at, at, f_send.at[first, chunk], f_recv.at[first, chunk], along_y[way])

    def forward_arrival(first, chunk):
        at = chunk_at(block_of(first), chunk, turn(y, 2, 4))
        return remote(at, at, f_send.at[first, chunk], f_recv.at[first, chunk], along_y[way_of(chunk)])

    def x_wait(first, chunk):
        at = chunk_at(block_of(first), chunk, y)
        remote(at, at, x_send.at[0, chunk], x_recv.at[first, chunk], partner).wait_recv()

    def y_start(first, chunk):
        for way in (way_of(chunk), 1 - way_of(chunk)):
            y_copy(way, first, chunk).start()

    def y_finish(first, side):
        for chunk in (2 * side, 2 * side + 1):
            y_arrival(1 - way_of(chunk), first, chunk).wait_recv()
            forward_arrival(first, chunk).wait_recv()

    def slot_of(way, hop):
        return {0: 0, 4: 1}.get(hop, 2 * hop + way)

    def z_copy(way, hop, sub):
        return remote(
            sub_at(slot_of(way, hop), sub), sub_at(slot_of(way, hop + 1), sub),
            z_send.at[way, hop, sub], z_recv.at[way, hop, sub], along_z[way],
        )

    def z_wait(way, hop, sub):
        at = sub_at(slot_of(way, hop), sub)
        remote(at, at, z_send.at[way, hop - 1, sub], z_recv.at[way, hop - 1, sub], along_z[way]).wait_recv()

    def z_step(hop, sub):
        for way in range(2):
            z_wait(way, hop, sub)
            if hop < 3 or sub % 2 == way:
                z_copy(way, hop, sub).start()

    def rows_of(group):
        return pl.ds(*group)

    def peer_copy(group, first):
        which, g = block_of(first), GROUPS.index(group)
        return remote(
            partial.at[1 - d, which, rows_of(group)], peer.at[which, rows_of(group)],
            p_send.at[first, g], p_recv.at[first, g], sibling,
        )

    def half_copy(group):
        g = GROUPS.index(group)
        return remote(
            half_out.at[rows_of(group)], half_in.at[rows_of(group)], q_send.at[g], q_recv.at[g], partner
        )

    def multiply_side(group, first, side):
        which = block_of(first)
        at = pl.multiple_of(which * SNAP + side * COLS, COLS)
        partial[side, which, rows_of(group)] = lax.dot_general(
            rows[rows_of(group), :], cols[pl.ds(at, COLS), :], (((1,), (1,)), ((), ())),
            preferred_element_type=jnp.float32,
        )

        @pl.when(d != side)
        def _():
            peer_copy(group, first).start()

    def multiply(group, first):
        for side in range(2):
            multiply_side(group, first, side)

    def sum_cores(group):
        peer_copy(group, 0).wait_recv()
        at = rows_of(group)
        half_out[at] = (partial[d, 1 - l, at] + peer[1 - l, at]).astype(jnp.bfloat16)
        half_copy(group).start()

    def sum_chips(group):
        peer_copy(group, 1).wait_recv()
        half_copy(group).wait_recv()
        at = rows_of(group)
        total = partial[d, l, at] + peer[l, at] + half_in[at].astype(jnp.float32)
        total = total * jnp.float32(1.0 / CELLS)
        for i in range(group[1] // STRIP):
            slot, sub = divmod(group[0] // STRIP + i, PIECE // STRIP)
            off = {0: 0, 1: 4}.get(slot, (-1, 1)[slot % 2] * (slot // 2))
            to = (sub % 2) * SNAP + (sub // 2) * CHUNK + turn(z, off, 8) * STRIP
            out_ref[pl.ds(pl.multiple_of(to, STRIP), STRIP), :] = total[i * STRIP : (i + 1) * STRIP]

    def z_first(chunk):
        for block in range(2):
            a_wait(chunk, block)
            for way in range(2):
                z_copy(way, 0, chunk * 2 + block).start()

    def y_second(chunk):
        @pl.when(inner)
        def _():
            x_wait(1, chunk)

        y_start(1, chunk)

    def y_first(chunk):
        x_wait(0, chunk)
        y_start(0, chunk)

    @pl.when(outer)
    def _():
        for chunk in range(CHUNKS):
            x_opposite(chunk, True).start()

    for chunk in range(CHUNKS):
        a_start(chunk)

    @pl.when(inner)
    def _():
        for chunk in range(CHUNKS):
            x_partner(chunk, False).start()
            x_opposite(chunk, False).start()

    for chunk in range(CHUNKS):
        z_first(chunk)
        x_relay(chunk)
        if chunk >= 2:
            y_second(chunk - 2)
    after = {
        (1, 1): [lambda: y_first(0)],
        (1, 3): [lambda: y_first(1)],
        (1, 5): [lambda: y_first(2)],
        (1, 7): [lambda: y_first(3)],
        (2, 0): [lambda: forward(0, 0)],
        (2, 1): [lambda: forward(0, 1)],
        (2, 2): [lambda: y_second(2), lambda: y_second(3)],
        (2, 3): [lambda: forward(0, 2), lambda: forward(1, 0)],
        (2, 4): [lambda: forward(0, 3)],
        (2, 5): [lambda: forward(1, 1)],
        (2, 7): [lambda: y_finish(0, 0), lambda: multiply_side(OWN, 0, 0)],
        (3, 0): [lambda: multiply_side(HOP1, 0, 0), lambda: y_finish(0, 1)],
        (3, 1): [lambda: multiply_side(OWN, 0, 1), lambda: forward(1, 2)],
        (3, 2): [lambda: multiply_side(HOP1, 0, 1), lambda: forward(1, 3)],
        (3, 3): [lambda: multiply_side(HOP2, 0, 0), lambda: sum_cores(OWN)],
        (3, 4): [lambda: multiply_side(HOP2, 0, 1), lambda: sum_cores(HOP1)],
        (3, 5): [lambda: y_finish(1, 0), lambda: multiply_side(OWN, 1, 0)],
        (3, 6): [lambda: multiply_side(HOP1, 1, 0)],
        (3, 7): [lambda: multiply_side(HOP2, 1, 0)],
    }
    for hop in range(1, 4):
        for sub in range(8):
            z_step(hop, sub)
            for action in after.get((hop, sub), ()):
                action()
    multiply(HOP3, 0)
    sum_cores(HOP2)
    multiply_side(HOP3, 1, 0)
    y_finish(1, 1)
    multiply_side(OWN, 1, 1)
    sum_cores(HOP3)
    for group in (HOP1, HOP2, HOP3):
        multiply_side(group, 1, 1)
    sum_chips(OWN)
    sum_chips(HOP1)
    for sub in range(8):
        z_wait(sub % 2, 4, sub)
    multiply(LAST, 0)
    multiply_side(LAST, 1, 0)
    sum_cores(LAST)
    multiply_side(LAST, 1, 1)
    sum_chips(HOP2)
    sum_chips(HOP3)
    sum_chips(LAST)

    for p in range(8):

        @pl.when(jnp.logical_not(stays(p)))
        def _():
            for chunk in range(CHUNKS):
                a_copy(chunk, p, False).wait_send()

    for chunk in range(CHUNKS):
        x_opposite(chunk, True).wait_send()
        x_partner(chunk, True).wait_send()
    for first in range(2):
        for chunk in range(CHUNKS):
            for way in range(2):
                y_copy(way, first, chunk).wait_send()
            forward_copy(first, chunk).wait_send()
    for way in range(2):
        for hop in range(4):
            for sub in range(8):
                if hop < 3 or sub % 2 == way:
                    z_copy(way, hop, sub).wait_send()
    for group in GROUPS:
        for first in range(2):
            peer_copy(group, first).wait_send()
        half_copy(group).wait_send()


def on_device(snapshots, cell_weight):
    hbm = pl.BlockSpec(memory_space=pltpu.HBM)
    dma = pltpu.SemaphoreType.DMA
    return pl.pallas_call(
        kernel,
        out_shape=jax.ShapeDtypeStruct((2 * SNAP, COLS), jnp.float32),
        in_specs=[hbm, hbm],
        out_specs=pl.BlockSpec(memory_space=pltpu.VMEM),
        scratch_shapes=[
            pltpu.VMEM((SNAP, CELL), jnp.bfloat16),
            pltpu.VMEM((CELL,), jnp.float32),
            pltpu.VMEM((SNAP, CELL), jnp.bfloat16),
            pltpu.VMEM((SNAP, CELL), jnp.bfloat16),
            pltpu.VMEM((2 * SNAP, 4 * CELL), jnp.bfloat16),
            pltpu.VMEM((8 * PIECE, 4 * CELL), jnp.bfloat16),
            pltpu.VMEM((2, 2, 8 * PIECE, COLS), jnp.float32),
            pltpu.VMEM((2, 8 * PIECE, COLS), jnp.float32),
            pltpu.VMEM((8 * PIECE, COLS), jnp.bfloat16),
            pltpu.VMEM((8 * PIECE, COLS), jnp.bfloat16),
            dma((2,)),
            dma((CHUNKS, 8)), dma((CHUNKS, 8)),
            dma((CHUNKS,)), dma((2, CHUNKS)), dma((2, CHUNKS)),
            dma((2, 2, CHUNKS)), dma((2, 2, CHUNKS)),
            dma((2, CHUNKS)), dma((2, CHUNKS)),
            dma((2, 4, 8)), dma((2, 4, 8)),
            dma((2, 6)), dma((2, 6)), dma((6,)), dma((6,)),
        ],
        compiler_params=pltpu.CompilerParams(
            collective_id=0, has_side_effects=True, vmem_limit_bytes=40 << 20
        ),
        name="gram",
    )(pltpu.with_memory_space_constraint(snapshots, pltpu.HBM), pltpu.with_memory_space_constraint(cell_weight, pltpu.HBM))


def solution(mesh):
    return jax.shard_map(
        on_device,
        mesh=mesh,
        in_specs=(P("col", ("row", "depth")), P(("row", "depth"))),
        out_specs=P("row", ("col", "depth")),
        check_vma=False,
    )
```

```python
import jax
import jax.numpy as jnp
from jax import lax
from jax.experimental import pallas as pl
from jax.experimental.pallas import tpu as pltpu
from jax.sharding import PartitionSpec as P

MESH = pl.DeviceIdType.MESH
CELLS = 6144
SNAP = 512
CELL = 384
PART = 64
PIECE = 2 * PART
COLS = 256
CHUNK = 128
CHUNKS = SNAP // CHUNK
STRIP = 16
SUBS = ((0, 1, 2, 3, 4, 5, 6, 7), (4, 5, 6, 7, 0, 1, 2, 3))

OWN, HOP1, HOP2, HOP3 = (0, PIECE), (2 * PIECE, 2 * PIECE), (4 * PIECE, 2 * PIECE), (6 * PIECE, 2 * PIECE)
LAST = (PIECE, PIECE)
GROUPS = (OWN, HOP1, HOP2, HOP3, LAST)


def kernel(
    snap_ref, weight_ref, out_ref, raw, weight, own, relay, cols, rows, partial, peer, half_out, half_in,
    in_sem, a_send, a_recv, r_recv, x_send, x_recv, y_send, y_recv, f_send, f_recv,
    z_send, z_recv, p_send, p_recv, q_send, q_recv,
):
    row, col, d = lax.axis_index("row"), lax.axis_index("col"), lax.axis_index("depth")
    h, y, l, z = row // 4, lax.rem(row, 4), col // 8, lax.rem(col, 8)

    def device(h, l, y, z, d):
        return (h * 4 + y, l * 8 + z, d)

    def turn(value, by, size):
        return lax.rem(value + by + size, size)

    along_y = [device(h, l, turn(y, by, 4), z, d) for by in (1, -1)]
    along_z = [device(h, l, y, turn(z, by, 8), d) for by in (1, -1)]
    sibling = device(h, l, y, z, 1 - d)
    partner = device(h, 1 - l, y, z, d)
    opposite = device(1 - h, 1 - l, y, z, d)
    outer = h == l
    inner = h != l

    load = [
        pltpu.make_async_copy(snap_ref, raw, in_sem.at[0]),
        pltpu.make_async_copy(weight_ref, weight, in_sem.at[1]),
    ]
    for copy in load:
        copy.start()

    barrier = pltpu.get_barrier_semaphore()

    def greet(target):
        pl.semaphore_signal(barrier, inc=1, device_id=target, device_id_type=MESH)

    for target in (opposite, partner, sibling, *along_y, *along_z):
        greet(target)
    for block in range(2):
        for part_y in range(4):
            greet(device(l, h, part_y, 2 * y + block, d))

    for copy in load:
        copy.wait()
    root = jnp.sqrt(weight[...])
    own[...] = (raw[...].astype(jnp.float32) * root[None, :]).astype(jnp.bfloat16)

    @pl.when(outer)
    def _():
        at = pl.ds(pl.multiple_of(l * SNAP, SNAP), SNAP), pl.ds(pl.multiple_of(y * CELL, CELL), CELL)
        cols[at] = own[...]

    pl.semaphore_wait(barrier, 15)

    def remote(src, dst, send, recv, target):
        return pltpu.make_async_remote_copy(
            src_ref=src, dst_ref=dst, send_sem=send, recv_sem=recv, device_id=target, device_id_type=MESH
        )

    def sub_at(slot, sub):
        return rows.at[pl.ds(slot * PIECE + sub * STRIP, STRIP), :]

    def chunk_at(which, chunk, cell_y):
        at = pl.multiple_of(which * SNAP + chunk * CHUNK, CHUNK)
        return cols.at[pl.ds(at, CHUNK), pl.ds(pl.multiple_of(cell_y * CELL, CELL), CELL)]

    def x_opposite(chunk, to_relay):
        src = own.at[pl.ds(chunk * CHUNK, CHUNK), :]
        if to_relay:
            return remote(src, relay.at[pl.ds(chunk * CHUNK, CHUNK), :], x_send.at[0, chunk], r_recv.at[chunk], opposite)
        return remote(src, chunk_at(l, chunk, y), x_send.at[0, chunk], x_recv.at[0, chunk], opposite)

    def x_partner(chunk, from_relay):
        if from_relay:
            src, which, first = relay.at[pl.ds(chunk * CHUNK, CHUNK), :], 1 - l, 1
        else:
            src, which, first = own.at[pl.ds(chunk * CHUNK, CHUNK), :], l, 0
        return remote(src, chunk_at(which, chunk, y), x_send.at[1, chunk], x_recv.at[first, chunk], partner)

    def x_relay(chunk):
        @pl.when(outer)
        def _():
            x_opposite(chunk, True).wait_recv()
            x_partner(chunk, True).start()

    half = lax.rem(z, 2)
    ring_y = z // 2
    a_index = half * 4 + y

    def stays(p):
        return outer & (y == ring_y) & (z == p)

    def a_copy(chunk, p, to_self):
        src = own.at[pl.ds(chunk * CHUNK + p * STRIP, STRIP), :]
        dst = rows.at[
            pl.ds(pl.multiple_of((2 * chunk + half) * STRIP, STRIP), STRIP),
            pl.ds(pl.multiple_of(y * CELL, CELL), CELL),
        ]
        recv = a_recv.at[chunk, a_index]
        if to_self:
            return pltpu.make_async_copy(src, dst, recv)
        return remote(src, dst, a_send.at[chunk, p], recv, device(l, h, ring_y, p, d))

    def a_start(chunk):
        for p in range(8):

            @pl.when(stays(p))
            def _():
                a_copy(chunk, p, True).start()

            @pl.when(jnp.logical_not(stays(p)))
            def _():
                a_copy(chunk, p, False).start()

    def a_wait(chunk, block):
        for cell_y in range(4):
            at = rows.at[pl.ds((2 * chunk + block) * STRIP, STRIP), pl.ds(cell_y * CELL, CELL)]
            remote(at, at, a_send.at[0, 0], a_recv.at[chunk, block * 4 + cell_y], partner).wait_recv()

    def block_of(turn_of):
        return 1 - l if turn_of == 0 else l

    def y_copy(way, first, chunk):
        at = chunk_at(block_of(first), chunk, y)
        return remote(at, at, y_send.at[way, first, chunk], y_recv.at[way, first, chunk], along_y[way])

    def y_arrival(way, first, chunk):
        at = chunk_at(block_of(first), chunk, turn(y, (-1, 1)[way], 4))
        return remote(at, at, y_send.at[way, first, chunk], y_recv.at[way, first, chunk], along_y[way])

    def way_of(chunk):
        return chunk % 2

    def forward(first, chunk):
        way = way_of(chunk)
        y_arrival(way, first, chunk).wait_recv()
        forward_copy(first, chunk).start()

    def forward_copy(first, chunk):
        way = way_of(chunk)
        at = chunk_at(block_of(first), chunk, turn(y, (-1, 1)[way], 4))
        return remote(at, at, f_send.at[first, chunk], f_recv.at[first, chunk], along_y[way])

    def forward_arrival(first, chunk):
        at = chunk_at(block_of(first), chunk, turn(y, 2, 4))
        return remote(at, at, f_send.at[first, chunk], f_recv.at[first, chunk], along_y[way_of(chunk)])

    def x_wait(first, chunk):
        at = chunk_at(block_of(first), chunk, y)
        remote(at, at, x_send.at[0, chunk], x_recv.at[first, chunk], partner).wait_recv()

    def y_start(first, chunk):
        for way in (way_of(chunk), 1 - way_of(chunk)):
            y_copy(way, first, chunk).start()

    def y_finish(first, side):
        for chunk in (2 * side, 2 * side + 1):
            y_arrival(1 - way_of(chunk), first, chunk).wait_recv()
            forward_arrival(first, chunk).wait_recv()

    def slot_of(way, hop):
        return {0: 0, 4: 1}.get(hop, 2 * hop + way)

    def z_copy(way, hop, sub):
        return remote(
            sub_at(slot_of(way, hop), sub), sub_at(slot_of(way, hop + 1), sub),
            z_send.at[way, hop, sub], z_recv.at[way, hop, sub], along_z[way],
        )

    def z_wait(way, hop, sub):
        at = sub_at(slot_of(way, hop), sub)
        remote(at, at, z_send.at[way, hop - 1, sub], z_recv.at[way, hop - 1, sub], along_z[way]).wait_recv()

    def z_step(hop, k):
        for way in range(2):
            z_wait(way, hop, SUBS[way][k])
            if hop < 3 or k < 4:
                z_copy(way, hop, SUBS[way][k]).start()

    def rows_of(group):
        return pl.ds(*group)

    def peer_copy(group, first):
        which, g = block_of(first), GROUPS.index(group)
        return remote(
            partial.at[1 - d, which, rows_of(group)], peer.at[which, rows_of(group)],
            p_send.at[first, g], p_recv.at[first, g], sibling,
        )

    def half_copy(group):
        g = GROUPS.index(group)
        return remote(
            half_out.at[rows_of(group)], half_in.at[rows_of(group)], q_send.at[g], q_recv.at[g], partner
        )

    def multiply_side(group, first, side):
        which = block_of(first)
        at = pl.multiple_of(which * SNAP + side * COLS, COLS)
        partial[side, which, rows_of(group)] = lax.dot_general(
            rows[rows_of(group), :], cols[pl.ds(at, COLS), :], (((1,), (1,)), ((), ())),
            preferred_element_type=jnp.float32,
        )

        @pl.when(d != side)
        def _():
            peer_copy(group, first).start()

    def multiply(group, first):
        for side in range(2):
            multiply_side(group, first, side)

    def sum_cores(group):
        peer_copy(group, 0).wait_recv()
        at = rows_of(group)
        half_out[at] = (partial[d, 1 - l, at] + peer[1 - l, at]).astype(jnp.bfloat16)
        half_copy(group).start()

    def sum_chips(group):
        peer_copy(group, 1).wait_recv()
        half_copy(group).wait_recv()
        at = rows_of(group)
        total = partial[d, l, at] + peer[l, at] + half_in[at].astype(jnp.float32)
        total = total * jnp.float32(1.0 / CELLS)
        for i in range(group[1] // STRIP):
            slot, sub = divmod(group[0] // STRIP + i, PIECE // STRIP)
            off = {0: 0, 1: 4}.get(slot, (-1, 1)[slot % 2] * (slot // 2))
            to = (sub % 2) * SNAP + (sub // 2) * CHUNK + turn(z, off, 8) * STRIP
            out_ref[pl.ds(pl.multiple_of(to, STRIP), STRIP), :] = total[i * STRIP : (i + 1) * STRIP]

    def z_first(way, ks):
        for k in ks:
            z_copy(way, 0, SUBS[way][k]).start()

    def y_second(chunk):
        @pl.when(inner)
        def _():
            x_wait(1, chunk)

        y_start(1, chunk)

    def y_first(chunk):
        x_wait(0, chunk)
        y_start(0, chunk)

    @pl.when(outer)
    def _():
        for chunk in range(CHUNKS):
            x_opposite(chunk, True).start()

    for chunk in (0, 2, 1, 3):
        a_start(chunk)

    @pl.when(inner)
    def _():
        for chunk in range(CHUNKS):
            x_partner(chunk, False).start()
            x_opposite(chunk, False).start()

    for i, chunk in enumerate((0, 2, 1, 3)):
        for block in range(2):
            a_wait(chunk, block)
        z_first(i % 2, (0, 1) if i < 2 else (2, 3))
        x_relay(i)
        if i >= 2:
            y_second(i - 2)
    for ks in ((4, 5), (6, 7)):
        for way in range(2):
            z_first(way, ks)
    after = {
        (1, 1): [lambda: y_first(0)],
        (1, 3): [lambda: y_first(1)],
        (1, 5): [lambda: y_first(2)],
        (1, 7): [lambda: y_first(3)],
        (2, 0): [lambda: forward(0, 0)],
        (2, 1): [lambda: forward(0, 1)],
        (2, 2): [lambda: y_second(2), lambda: y_second(3)],
        (2, 3): [lambda: forward(0, 2), lambda: forward(1, 0)],
        (2, 4): [lambda: forward(0, 3)],
        (2, 5): [lambda: forward(1, 1)],
        (2, 7): [lambda: y_finish(0, 0), lambda: multiply_side(OWN, 0, 0)],
        (3, 0): [lambda: multiply_side(HOP1, 0, 0), lambda: y_finish(0, 1)],
        (3, 1): [lambda: multiply_side(OWN, 0, 1), lambda: forward(1, 2)],
        (3, 2): [lambda: multiply_side(HOP1, 0, 1), lambda: forward(1, 3)],
        (3, 3): [lambda: multiply_side(HOP2, 0, 0), lambda: sum_cores(OWN)],
        (3, 4): [lambda: multiply_side(HOP2, 0, 1)],
        (3, 5): [lambda: sum_cores(HOP1)],
        (3, 6): [lambda: sum_cores(HOP2)],
    }
    for hop in range(1, 4):
        for sub in range(8):
            z_step(hop, sub)
            for action in after.get((hop, sub), ()):
                action()
    multiply(HOP3, 0)
    y_finish(1, 0)
    multiply_side(OWN, 1, 0)
    multiply_side(HOP1, 1, 0)
    sum_cores(HOP3)
    y_finish(1, 1)
    multiply_side(OWN, 1, 1)
    multiply_side(HOP1, 1, 1)
    multiply(HOP2, 1)
    for sub in range(8):
        z_wait(sub // 4, 4, sub)
    multiply(LAST, 0)
    multiply(HOP3, 1)
    sum_cores(LAST)
    multiply(LAST, 1)
    for group in GROUPS:
        sum_chips(group)
    for p in range(8):

        @pl.when(jnp.logical_not(stays(p)))
        def _():
            for chunk in range(CHUNKS):
                a_copy(chunk, p, False).wait_send()

    for chunk in range(CHUNKS):
        x_opposite(chunk, True).wait_send()
        x_partner(chunk, True).wait_send()
    for first in range(2):
        for chunk in range(CHUNKS):
            for way in range(2):
                y_copy(way, first, chunk).wait_send()
            forward_copy(first, chunk).wait_send()
    for way in range(2):
        for hop in range(4):
            for sub in range(8):
                if hop < 3 or sub // 4 == way:
                    z_copy(way, hop, sub).wait_send()
    for group in GROUPS:
        for first in range(2):
            peer_copy(group, first).wait_send()
        half_copy(group).wait_send()


def on_device(snapshots, cell_weight):
    hbm = pl.BlockSpec(memory_space=pltpu.HBM)
    dma = pltpu.SemaphoreType.DMA
    return pl.pallas_call(
        kernel,
        out_shape=jax.ShapeDtypeStruct((2 * SNAP, COLS), jnp.float32),
        in_specs=[hbm, hbm],
        out_specs=pl.BlockSpec(memory_space=pltpu.VMEM),
        scratch_shapes=[
            pltpu.VMEM((SNAP, CELL), jnp.bfloat16),
            pltpu.VMEM((CELL,), jnp.float32),
            pltpu.VMEM((SNAP, CELL), jnp.bfloat16),
            pltpu.VMEM((SNAP, CELL), jnp.bfloat16),
            pltpu.VMEM((2 * SNAP, 4 * CELL), jnp.bfloat16),
            pltpu.VMEM((8 * PIECE, 4 * CELL), jnp.bfloat16),
            pltpu.VMEM((2, 2, 8 * PIECE, COLS), jnp.float32),
            pltpu.VMEM((2, 8 * PIECE, COLS), jnp.float32),
            pltpu.VMEM((8 * PIECE, COLS), jnp.bfloat16),
            pltpu.VMEM((8 * PIECE, COLS), jnp.bfloat16),
            dma((2,)),
            dma((CHUNKS, 8)), dma((CHUNKS, 8)),
            dma((CHUNKS,)), dma((2, CHUNKS)), dma((2, CHUNKS)),
            dma((2, 2, CHUNKS)), dma((2, 2, CHUNKS)),
            dma((2, CHUNKS)), dma((2, CHUNKS)),
            dma((2, 4, 8)), dma((2, 4, 8)),
            dma((2, 6)), dma((2, 6)), dma((6,)), dma((6,)),
        ],
        compiler_params=pltpu.CompilerParams(
            collective_id=0, has_side_effects=True, vmem_limit_bytes=40 << 20
        ),
        name="gram",
    )(pltpu.with_memory_space_constraint(snapshots, pltpu.HBM), pltpu.with_memory_space_constraint(cell_weight, pltpu.HBM))


def solution(mesh):
    return jax.shard_map(
        on_device,
        mesh=mesh,
        in_specs=(P("col", ("row", "depth")), P(("row", "depth"))),
        out_specs=P("row", ("col", "depth")),
        check_vma=False,
    )
```

```python
import jax
import jax.numpy as jnp
from jax import lax
from jax.experimental import pallas as pl
from jax.experimental.pallas import tpu as pltpu
from jax.sharding import PartitionSpec as P

MESH = pl.DeviceIdType.MESH
CELLS = 6144
SNAP = 512
CELL = 384
PART = 64
PIECE = 2 * PART
COLS = 256
CHUNK = 128
CHUNKS = SNAP // CHUNK
STRIP = 16
SUBS = ((0, 1, 2, 3, 4, 5, 6, 7), (4, 5, 6, 7, 0, 1, 2, 3))

OWN, HOP1, HOP2, HOP3 = (0, PIECE), (2 * PIECE, 2 * PIECE), (4 * PIECE, 2 * PIECE), (6 * PIECE, 2 * PIECE)
LAST = (PIECE, PIECE)
GROUPS = (OWN, HOP1, HOP2, HOP3, LAST)


def kernel(
    snap_ref, weight_ref, out_ref, raw, weight, own, relay, cols, rows, partial, peer, half_out, half_in,
    in_sem, a_send, a_recv, r_recv, x_send, x_recv, y_send, y_recv, f_send, f_recv,
    z_send, z_recv, p_send, p_recv, q_send, q_recv,
):
    row, col, d = lax.axis_index("row"), lax.axis_index("col"), lax.axis_index("depth")
    h, y, l, z = row // 4, lax.rem(row, 4), col // 8, lax.rem(col, 8)

    def device(h, l, y, z, d):
        return (h * 4 + y, l * 8 + z, d)

    def turn(value, by, size):
        return lax.rem(value + by + size, size)

    along_y = [device(h, l, turn(y, by, 4), z, d) for by in (1, -1)]
    along_z = [device(h, l, y, turn(z, by, 8), d) for by in (1, -1)]
    sibling = device(h, l, y, z, 1 - d)
    partner = device(h, 1 - l, y, z, d)
    opposite = device(1 - h, 1 - l, y, z, d)
    outer = h == l
    inner = h != l

    load = [
        pltpu.make_async_copy(snap_ref, raw, in_sem.at[0]),
        pltpu.make_async_copy(weight_ref, weight, in_sem.at[1]),
    ]
    for copy in load:
        copy.start()

    barrier = pltpu.get_barrier_semaphore()

    def greet(target):
        pl.semaphore_signal(barrier, inc=1, device_id=target, device_id_type=MESH)

    for target in (opposite, partner, sibling, *along_y, *along_z):
        greet(target)
    for block in range(2):
        for part_y in range(4):
            greet(device(l, h, part_y, 2 * y + block, d))

    for copy in load:
        copy.wait()
    root = jnp.sqrt(weight[...])
    own[...] = (raw[...].astype(jnp.float32) * root[None, :]).astype(jnp.bfloat16)

    @pl.when(outer)
    def _():
        at = pl.ds(pl.multiple_of(l * SNAP, SNAP), SNAP), pl.ds(pl.multiple_of(y * CELL, CELL), CELL)
        cols[at] = own[...]

    pl.semaphore_wait(barrier, 15)

    def remote(src, dst, send, recv, target):
        return pltpu.make_async_remote_copy(
            src_ref=src, dst_ref=dst, send_sem=send, recv_sem=recv, device_id=target, device_id_type=MESH
        )

    def sub_at(slot, sub):
        return rows.at[pl.ds(slot * PIECE + sub * STRIP, STRIP), :]

    def chunk_at(which, chunk, cell_y):
        at = pl.multiple_of(which * SNAP + chunk * CHUNK, CHUNK)
        return cols.at[pl.ds(at, CHUNK), pl.ds(pl.multiple_of(cell_y * CELL, CELL), CELL)]

    def x_opposite(chunk, to_relay):
        src = own.at[pl.ds(chunk * CHUNK, CHUNK), :]
        if to_relay:
            return remote(src, relay.at[pl.ds(chunk * CHUNK, CHUNK), :], x_send.at[0, chunk], r_recv.at[chunk], opposite)
        return remote(src, chunk_at(l, chunk, y), x_send.at[0, chunk], x_recv.at[0, chunk], opposite)

    def x_partner(chunk, from_relay):
        if from_relay:
            src, which, first = relay.at[pl.ds(chunk * CHUNK, CHUNK), :], 1 - l, 1
        else:
            src, which, first = own.at[pl.ds(chunk * CHUNK, CHUNK), :], l, 0
        return remote(src, chunk_at(which, chunk, y), x_send.at[1, chunk], x_recv.at[first, chunk], partner)

    def x_relay(chunk):
        @pl.when(outer)
        def _():
            x_opposite(chunk, True).wait_recv()
            x_partner(chunk, True).start()

    half = lax.rem(z, 2)
    ring_y = z // 2
    a_index = half * 4 + y

    def stays(p):
        return outer & (y == ring_y) & (z == p)

    def a_copy(chunk, p, to_self):
        src = own.at[pl.ds(chunk * CHUNK + p * STRIP, STRIP), :]
        dst = rows.at[
            pl.ds(pl.multiple_of((2 * chunk + half) * STRIP, STRIP), STRIP),
            pl.ds(pl.multiple_of(y * CELL, CELL), CELL),
        ]
        recv = a_recv.at[chunk, a_index]
        if to_self:
            return pltpu.make_async_copy(src, dst, recv)
        return remote(src, dst, a_send.at[chunk, p], recv, device(l, h, ring_y, p, d))

    def a_start(chunk):
        for p in range(8):

            @pl.when(stays(p))
            def _():
                a_copy(chunk, p, True).start()

            @pl.when(jnp.logical_not(stays(p)))
            def _():
                a_copy(chunk, p, False).start()

    def a_wait(chunk, block):
        for cell_y in range(4):
            at = rows.at[pl.ds((2 * chunk + block) * STRIP, STRIP), pl.ds(cell_y * CELL, CELL)]
            remote(at, at, a_send.at[0, 0], a_recv.at[chunk, block * 4 + cell_y], partner).wait_recv()

    def block_of(turn_of):
        return 1 - l if turn_of == 0 else l

    def y_copy(way, first, chunk):
        at = chunk_at(block_of(first), chunk, y)
        return remote(at, at, y_send.at[way, first, chunk], y_recv.at[way, first, chunk], along_y[way])

    def y_arrival(way, first, chunk):
        at = chunk_at(block_of(first), chunk, turn(y, (-1, 1)[way], 4))
        return remote(at, at, y_send.at[way, first, chunk], y_recv.at[way, first, chunk], along_y[way])

    def way_of(chunk):
        return chunk % 2

    def forward(first, chunk):
        way = way_of(chunk)
        y_arrival(way, first, chunk).wait_recv()
        forward_copy(first, chunk).start()

    def forward_copy(first, chunk):
        way = way_of(chunk)
        at = chunk_at(block_of(first), chunk, turn(y, (-1, 1)[way], 4))
        return remote(at, at, f_send.at[first, chunk], f_recv.at[first, chunk], along_y[way])

    def forward_arrival(first, chunk):
        at = chunk_at(block_of(first), chunk, turn(y, 2, 4))
        return remote(at, at, f_send.at[first, chunk], f_recv.at[first, chunk], along_y[way_of(chunk)])

    def x_wait(first, chunk):
        at = chunk_at(block_of(first), chunk, y)
        remote(at, at, x_send.at[0, chunk], x_recv.at[first, chunk], partner).wait_recv()

    def y_start(first, chunk):
        for way in (way_of(chunk), 1 - way_of(chunk)):
            y_copy(way, first, chunk).start()

    def y_finish(first, side):
        for chunk in (2 * side, 2 * side + 1):
            y_arrival(1 - way_of(chunk), first, chunk).wait_recv()
            forward_arrival(first, chunk).wait_recv()

    def slot_of(way, hop):
        return {0: 0, 4: 1}.get(hop, 2 * hop + way)

    def z_copy(way, hop, sub):
        return remote(
            sub_at(slot_of(way, hop), sub), sub_at(slot_of(way, hop + 1), sub),
            z_send.at[way, hop, sub], z_recv.at[way, hop, sub], along_z[way],
        )

    def z_wait(way, hop, sub):
        at = sub_at(slot_of(way, hop), sub)
        remote(at, at, z_send.at[way, hop - 1, sub], z_recv.at[way, hop - 1, sub], along_z[way]).wait_recv()

    def z_step(hop, k):
        for way in range(2):
            z_wait(way, hop, SUBS[way][k])
            if hop < 3 or k < 4:
                z_copy(way, hop, SUBS[way][k]).start()

    def rows_of(group):
        return pl.ds(*group)

    def peer_copy(group, first):
        which, g = block_of(first), GROUPS.index(group)
        return remote(
            partial.at[1 - d, which, rows_of(group)], peer.at[which, rows_of(group)],
            p_send.at[first, g], p_recv.at[first, g], sibling,
        )

    def half_copy(group):
        g = GROUPS.index(group)
        return remote(
            half_out.at[rows_of(group)], half_in.at[rows_of(group)], q_send.at[g], q_recv.at[g], partner
        )

    def multiply_side(group, first, side):
        which = block_of(first)
        at = pl.multiple_of(which * SNAP + side * COLS, COLS)
        partial[side, which, rows_of(group)] = lax.dot_general(
            rows[rows_of(group), :], cols[pl.ds(at, COLS), :], (((1,), (1,)), ((), ())),
            preferred_element_type=jnp.float32,
        )

        @pl.when(d != side)
        def _():
            peer_copy(group, first).start()

    def multiply_urgent(group):
        which = block_of(0)
        for side in (1 - d, d):
            at = pl.multiple_of(which * SNAP + side * COLS, COLS)
            partial[side, which, rows_of(group)] = lax.dot_general(
                rows[rows_of(group), :], cols[pl.ds(at, COLS), :], (((1,), (1,)), ((), ())),
                preferred_element_type=jnp.float32,
            )
            if side is not d:
                peer_copy(group, 0).start()

    def multiply(group, first):
        for side in range(2):
            multiply_side(group, first, side)

    def sum_cores(group):
        peer_copy(group, 0).wait_recv()
        at = rows_of(group)
        half_out[at] = (partial[d, 1 - l, at] + peer[1 - l, at]).astype(jnp.bfloat16)
        half_copy(group).start()

    def sum_chips(group):
        peer_copy(group, 1).wait_recv()
        half_copy(group).wait_recv()
        at = rows_of(group)
        total = partial[d, l, at] + peer[l, at] + half_in[at].astype(jnp.float32)
        total = total * jnp.float32(1.0 / CELLS)
        for i in range(group[1] // STRIP):
            slot, sub = divmod(group[0] // STRIP + i, PIECE // STRIP)
            off = {0: 0, 1: 4}.get(slot, (-1, 1)[slot % 2] * (slot // 2))
            to = (sub % 2) * SNAP + (sub // 2) * CHUNK + turn(z, off, 8) * STRIP
            out_ref[pl.ds(pl.multiple_of(to, STRIP), STRIP), :] = total[i * STRIP : (i + 1) * STRIP]

    def z_first(way, ks):
        for k in ks:
            z_copy(way, 0, SUBS[way][k]).start()

    def y_second(chunk):
        @pl.when(inner)
        def _():
            x_wait(1, chunk)

        y_start(1, chunk)

    def y_first(chunk):
        x_wait(0, chunk)
        y_start(0, chunk)

    @pl.when(outer)
    def _():
        for chunk in range(CHUNKS):
            x_opposite(chunk, True).start()

    for chunk in (0, 2, 1, 3):
        a_start(chunk)

    @pl.when(inner)
    def _():
        for chunk in range(CHUNKS):
            x_partner(chunk, False).start()
            x_opposite(chunk, False).start()

    for i, chunk in enumerate((0, 2, 1, 3)):
        for block in range(2):
            a_wait(chunk, block)
        z_first(i % 2, (0, 1) if i < 2 else (2, 3))
        x_relay(i)
        if i >= 2:
            y_second(i - 2)
    for ks in ((4, 5), (6, 7)):
        for way in range(2):
            z_first(way, ks)
    after = {
        (1, 1): [lambda: y_first(0)],
        (1, 3): [lambda: y_first(1)],
        (1, 5): [lambda: y_first(2)],
        (1, 7): [lambda: y_first(3)],
        (2, 0): [lambda: forward(0, 0)],
        (2, 1): [lambda: forward(0, 1)],
        (2, 2): [lambda: y_second(2), lambda: y_second(3)],
        (2, 3): [lambda: forward(0, 2), lambda: forward(1, 0)],
        (2, 4): [lambda: forward(0, 3)],
        (2, 5): [lambda: forward(1, 1)],
        (2, 7): [lambda: y_finish(0, 0), lambda: multiply_side(OWN, 0, 0)],
        (3, 0): [lambda: multiply_side(HOP1, 0, 0), lambda: y_finish(0, 1)],
        (3, 1): [lambda: multiply_side(OWN, 0, 1), lambda: forward(1, 2)],
        (3, 2): [lambda: multiply_side(HOP1, 0, 1), lambda: forward(1, 3)],
        (3, 3): [lambda: multiply_side(HOP2, 0, 0), lambda: sum_cores(OWN)],
        (3, 4): [lambda: multiply_side(HOP2, 0, 1)],
        (3, 5): [lambda: sum_cores(HOP1)],
        (3, 6): [lambda: sum_cores(HOP2)],
    }
    for hop in range(1, 4):
        for sub in range(8):
            z_step(hop, sub)
            for action in after.get((hop, sub), ()):
                action()
    multiply_urgent(HOP3)
    y_finish(1, 0)
    multiply_side(OWN, 1, 0)
    multiply_side(HOP1, 1, 0)
    sum_cores(HOP3)
    y_finish(1, 1)
    multiply_side(OWN, 1, 1)
    multiply_side(HOP1, 1, 1)
    multiply(HOP2, 1)
    for sub in range(8):
        z_wait(sub // 4, 4, sub)
    multiply_urgent(LAST)
    multiply(HOP3, 1)
    sum_cores(LAST)
    multiply(LAST, 1)
    for group in GROUPS:
        sum_chips(group)
    for p in range(8):

        @pl.when(jnp.logical_not(stays(p)))
        def _():
            for chunk in range(CHUNKS):
                a_copy(chunk, p, False).wait_send()

    for chunk in range(CHUNKS):
        x_opposite(chunk, True).wait_send()
        x_partner(chunk, True).wait_send()
    for first in range(2):
        for chunk in range(CHUNKS):
            for way in range(2):
                y_copy(way, first, chunk).wait_send()
            forward_copy(first, chunk).wait_send()
    for way in range(2):
        for hop in range(4):
            for sub in range(8):
                if hop < 3 or sub // 4 == way:
                    z_copy(way, hop, sub).wait_send()
    for group in GROUPS:
        for first in range(2):
            peer_copy(group, first).wait_send()
        half_copy(group).wait_send()


def on_device(snapshots, cell_weight):
    hbm = pl.BlockSpec(memory_space=pltpu.HBM)
    dma = pltpu.SemaphoreType.DMA
    return pl.pallas_call(
        kernel,
        out_shape=jax.ShapeDtypeStruct((2 * SNAP, COLS), jnp.float32),
        in_specs=[hbm, hbm],
        out_specs=pl.BlockSpec(memory_space=pltpu.VMEM),
        scratch_shapes=[
            pltpu.VMEM((SNAP, CELL), jnp.bfloat16),
            pltpu.VMEM((CELL,), jnp.float32),
            pltpu.VMEM((SNAP, CELL), jnp.bfloat16),
            pltpu.VMEM((SNAP, CELL), jnp.bfloat16),
            pltpu.VMEM((2 * SNAP, 4 * CELL), jnp.bfloat16),
            pltpu.VMEM((8 * PIECE, 4 * CELL), jnp.bfloat16),
            pltpu.VMEM((2, 2, 8 * PIECE, COLS), jnp.float32),
            pltpu.VMEM((2, 8 * PIECE, COLS), jnp.float32),
            pltpu.VMEM((8 * PIECE, COLS), jnp.bfloat16),
            pltpu.VMEM((8 * PIECE, COLS), jnp.bfloat16),
            dma((2,)),
            dma((CHUNKS, 8)), dma((CHUNKS, 8)),
            dma((CHUNKS,)), dma((2, CHUNKS)), dma((2, CHUNKS)),
            dma((2, 2, CHUNKS)), dma((2, 2, CHUNKS)),
            dma((2, CHUNKS)), dma((2, CHUNKS)),
            dma((2, 4, 8)), dma((2, 4, 8)),
            dma((2, 6)), dma((2, 6)), dma((6,)), dma((6,)),
        ],
        compiler_params=pltpu.CompilerParams(
            collective_id=0, has_side_effects=True, vmem_limit_bytes=40 << 20
        ),
        name="gram",
    )(pltpu.with_memory_space_constraint(snapshots, pltpu.HBM), pltpu.with_memory_space_constraint(cell_weight, pltpu.HBM))


def solution(mesh):
    return jax.shard_map(
        on_device,
        mesh=mesh,
        in_specs=(P("col", ("row", "depth")), P(("row", "depth"))),
        out_specs=P("row", ("col", "depth")),
        check_vma=False,
    )
```

```python
import jax
import jax.numpy as jnp
from jax import lax
from jax.experimental import pallas as pl
from jax.experimental.pallas import tpu as pltpu
from jax.sharding import PartitionSpec as P

MESH = pl.DeviceIdType.MESH
CELLS = 6144
SNAP = 512
CELL = 384
PART = 64
PIECE = 2 * PART
COLS = 256
CHUNK = 128
CHUNKS = SNAP // CHUNK
STRIP = 16
SUBS = ((0, 1, 2, 3, 4, 5, 6, 7), (4, 5, 6, 7, 0, 1, 2, 3))

OWN, HOP1, HOP2, HOP3 = (0, PIECE), (2 * PIECE, 2 * PIECE), (4 * PIECE, 2 * PIECE), (6 * PIECE, 2 * PIECE)
LAST = (PIECE, PIECE)
GROUPS = (OWN, HOP1, HOP2, HOP3, LAST)


def kernel(
    snap_ref, weight_ref, out_ref, raw, weight, own, relay, cols, rows, partial, peer, half_out, half_in,
    in_sem, a_send, a_recv, r_recv, x_send, x_recv, y_send, y_recv, f_send, f_recv,
    z_send, z_recv, p_send, p_recv, q_send, q_recv,
):
    row, col, d = lax.axis_index("row"), lax.axis_index("col"), lax.axis_index("depth")
    h, y, l, z = row // 4, lax.rem(row, 4), col // 8, lax.rem(col, 8)

    def device(h, l, y, z, d):
        return (h * 4 + y, l * 8 + z, d)

    def turn(value, by, size):
        return lax.rem(value + by + size, size)

    along_y = [device(h, l, turn(y, by, 4), z, d) for by in (1, -1)]
    along_z = [device(h, l, y, turn(z, by, 8), d) for by in (1, -1)]
    sibling = device(h, l, y, z, 1 - d)
    partner = device(h, 1 - l, y, z, d)
    opposite = device(1 - h, 1 - l, y, z, d)
    outer = h == l
    inner = h != l

    load = [
        pltpu.make_async_copy(snap_ref, raw, in_sem.at[0]),
        pltpu.make_async_copy(weight_ref, weight, in_sem.at[1]),
    ]
    for copy in load:
        copy.start()

    barrier = pltpu.get_barrier_semaphore()

    def greet(target):
        pl.semaphore_signal(barrier, inc=1, device_id=target, device_id_type=MESH)

    for target in (opposite, partner, sibling, *along_y, *along_z):
        greet(target)
    for block in range(2):
        for part_y in range(4):
            greet(device(l, h, part_y, 2 * y + block, d))

    for copy in load:
        copy.wait()
    root = jnp.sqrt(weight[...])
    own[...] = (raw[...].astype(jnp.float32) * root[None, :]).astype(jnp.bfloat16)

    @pl.when(outer)
    def _():
        at = pl.ds(pl.multiple_of(l * SNAP, SNAP), SNAP), pl.ds(pl.multiple_of(y * CELL, CELL), CELL)
        cols[at] = own[...]

    pl.semaphore_wait(barrier, 15)

    def remote(src, dst, send, recv, target):
        return pltpu.make_async_remote_copy(
            src_ref=src, dst_ref=dst, send_sem=send, recv_sem=recv, device_id=target, device_id_type=MESH
        )

    def sub_at(slot, sub):
        return rows.at[pl.ds(slot * PIECE + sub * STRIP, STRIP), :]

    def chunk_at(which, chunk, cell_y):
        at = pl.multiple_of(which * SNAP + chunk * CHUNK, CHUNK)
        return cols.at[pl.ds(at, CHUNK), pl.ds(pl.multiple_of(cell_y * CELL, CELL), CELL)]

    def x_opposite(chunk, to_relay):
        src = own.at[pl.ds(chunk * CHUNK, CHUNK), :]
        if to_relay:
            return remote(src, relay.at[pl.ds(chunk * CHUNK, CHUNK), :], x_send.at[0, chunk], r_recv.at[chunk], opposite)
        return remote(src, chunk_at(l, chunk, y), x_send.at[0, chunk], x_recv.at[0, chunk], opposite)

    def x_partner(chunk, from_relay):
        if from_relay:
            src, which, first = relay.at[pl.ds(chunk * CHUNK, CHUNK), :], 1 - l, 1
        else:
            src, which, first = own.at[pl.ds(chunk * CHUNK, CHUNK), :], l, 0
        return remote(src, chunk_at(which, chunk, y), x_send.at[1, chunk], x_recv.at[first, chunk], partner)

    def x_relay(chunk):
        @pl.when(outer)
        def _():
            x_opposite(chunk, True).wait_recv()
            x_partner(chunk, True).start()

    half = lax.rem(z, 2)
    ring_y = z // 2
    a_index = half * 4 + y

    def stays(p):
        return outer & (y == ring_y) & (z == p)

    def a_copy(chunk, p, to_self):
        src = own.at[pl.ds(chunk * CHUNK + p * STRIP, STRIP), :]
        dst = rows.at[
            pl.ds(pl.multiple_of((2 * chunk + half) * STRIP, STRIP), STRIP),
            pl.ds(pl.multiple_of(y * CELL, CELL), CELL),
        ]
        recv = a_recv.at[chunk, a_index]
        if to_self:
            return pltpu.make_async_copy(src, dst, recv)
        return remote(src, dst, a_send.at[chunk, p], recv, device(l, h, ring_y, p, d))

    def a_start(chunk):
        for p in range(8):

            @pl.when(stays(p))
            def _():
                a_copy(chunk, p, True).start()

            @pl.when(jnp.logical_not(stays(p)))
            def _():
                a_copy(chunk, p, False).start()

    def a_wait(chunk, block):
        for cell_y in range(4):
            at = rows.at[pl.ds((2 * chunk + block) * STRIP, STRIP), pl.ds(cell_y * CELL, CELL)]
            remote(at, at, a_send.at[0, 0], a_recv.at[chunk, block * 4 + cell_y], partner).wait_recv()

    def block_of(turn_of):
        return 1 - l if turn_of == 0 else l

    def y_copy(way, first, chunk):
        at = chunk_at(block_of(first), chunk, y)
        return remote(at, at, y_send.at[way, first, chunk], y_recv.at[way, first, chunk], along_y[way])

    def y_arrival(way, first, chunk):
        at = chunk_at(block_of(first), chunk, turn(y, (-1, 1)[way], 4))
        return remote(at, at, y_send.at[way, first, chunk], y_recv.at[way, first, chunk], along_y[way])

    def way_of(chunk):
        return chunk % 2

    def forward(first, chunk):
        way = way_of(chunk)
        y_arrival(way, first, chunk).wait_recv()
        forward_copy(first, chunk).start()

    def forward_copy(first, chunk):
        way = way_of(chunk)
        at = chunk_at(block_of(first), chunk, turn(y, (-1, 1)[way], 4))
        return remote(at, at, f_send.at[first, chunk], f_recv.at[first, chunk], along_y[way])

    def forward_arrival(first, chunk):
        at = chunk_at(block_of(first), chunk, turn(y, 2, 4))
        return remote(at, at, f_send.at[first, chunk], f_recv.at[first, chunk], along_y[way_of(chunk)])

    def x_wait(first, chunk):
        at = chunk_at(block_of(first), chunk, y)
        remote(at, at, x_send.at[0, chunk], x_recv.at[first, chunk], partner).wait_recv()

    def y_start(first, chunk):
        for way in (way_of(chunk), 1 - way_of(chunk)):
            y_copy(way, first, chunk).start()

    def y_finish(first, side):
        for chunk in (2 * side, 2 * side + 1):
            y_arrival(1 - way_of(chunk), first, chunk).wait_recv()
            forward_arrival(first, chunk).wait_recv()

    def slot_of(way, hop):
        return {0: 0, 4: 1}.get(hop, 2 * hop + way)

    def z_copy(way, hop, sub):
        return remote(
            sub_at(slot_of(way, hop), sub), sub_at(slot_of(way, hop + 1), sub),
            z_send.at[way, hop, sub], z_recv.at[way, hop, sub], along_z[way],
        )

    def z_wait(way, hop, sub):
        at = sub_at(slot_of(way, hop), sub)
        remote(at, at, z_send.at[way, hop - 1, sub], z_recv.at[way, hop - 1, sub], along_z[way]).wait_recv()

    def z_step(hop, k):
        for way in range(2):
            z_wait(way, hop, SUBS[way][k])
            if hop < 3 or k < 4:
                z_copy(way, hop, SUBS[way][k]).start()

    def rows_of(group):
        return pl.ds(*group)

    def peer_copy(group, first):
        which, g = block_of(first), GROUPS.index(group)
        return remote(
            partial.at[1 - d, which, rows_of(group)], peer.at[which, rows_of(group)],
            p_send.at[first, g], p_recv.at[first, g], sibling,
        )

    def half_copy(group):
        g = GROUPS.index(group)
        return remote(
            half_out.at[rows_of(group)], half_in.at[rows_of(group)], q_send.at[g], q_recv.at[g], partner
        )

    def multiply_side(group, first, side):
        which = block_of(first)
        at = pl.multiple_of(which * SNAP + side * COLS, COLS)
        partial[side, which, rows_of(group)] = lax.dot_general(
            rows[rows_of(group), :], cols[pl.ds(at, COLS), :], (((1,), (1,)), ((), ())),
            preferred_element_type=jnp.float32,
        )

        @pl.when(d != side)
        def _():
            peer_copy(group, first).start()

    def multiply_urgent(group):
        which = block_of(0)
        for side in (1 - d, d):
            at = pl.multiple_of(which * SNAP + side * COLS, COLS)
            partial[side, which, rows_of(group)] = lax.dot_general(
                rows[rows_of(group), :], cols[pl.ds(at, COLS), :], (((1,), (1,)), ((), ())),
                preferred_element_type=jnp.float32,
            )
            if side is not d:
                peer_copy(group, 0).start()

    def multiply(group, first):
        for side in range(2):
            multiply_side(group, first, side)

    def sum_cores(group):
        peer_copy(group, 0).wait_recv()
        at = rows_of(group)
        half_out[at] = (partial[d, 1 - l, at] + peer[1 - l, at]).astype(jnp.bfloat16)
        half_copy(group).start()

    def sum_chips(group):
        peer_copy(group, 1).wait_recv()
        half_copy(group).wait_recv()
        at = rows_of(group)
        total = partial[d, l, at] + peer[l, at] + half_in[at].astype(jnp.float32)
        total = total * jnp.float32(1.0 / CELLS)
        for i in range(group[1] // STRIP):
            slot, sub = divmod(group[0] // STRIP + i, PIECE // STRIP)
            off = {0: 0, 1: 4}.get(slot, (-1, 1)[slot % 2] * (slot // 2))
            to = (sub % 2) * SNAP + (sub // 2) * CHUNK + turn(z, off, 8) * STRIP
            out_ref[pl.ds(pl.multiple_of(to, STRIP), STRIP), :] = total[i * STRIP : (i + 1) * STRIP]

    def z_first(way, ks):
        for k in ks:
            z_copy(way, 0, SUBS[way][k]).start()

    def y_second(chunk):
        @pl.when(inner)
        def _():
            x_wait(1, chunk)

        y_start(1, chunk)

    def y_first(chunk):
        x_wait(0, chunk)
        y_start(0, chunk)

    @pl.when(outer)
    def _():
        for chunk in range(CHUNKS):
            x_opposite(chunk, True).start()

    for chunk in (0, 2, 1, 3):
        a_start(chunk)

    @pl.when(inner)
    def _():
        for chunk in range(CHUNKS):
            x_partner(chunk, False).start()
            x_opposite(chunk, False).start()

    for i, chunk in enumerate((0, 2, 1, 3)):
        for block in range(2):
            a_wait(chunk, block)
        z_first(i % 2, (0, 1) if i < 2 else (2, 3))
        x_relay(i)
        if i >= 2:
            y_second(i - 2)
    for ks in ((4, 5), (6, 7)):
        for way in range(2):
            z_first(way, ks)
    after = {
        (1, 1): [lambda: y_first(0)],
        (1, 3): [lambda: y_first(1)],
        (1, 5): [lambda: y_first(2)],
        (1, 7): [lambda: y_first(3)],
        (2, 0): [lambda: forward(0, 0)],
        (2, 1): [lambda: forward(0, 1)],
        (2, 2): [lambda: y_second(2), lambda: y_second(3)],
        (2, 3): [lambda: forward(0, 2), lambda: forward(1, 0)],
        (2, 4): [lambda: forward(0, 3)],
        (2, 5): [lambda: forward(1, 1)],
        (2, 7): [lambda: y_finish(0, 0), lambda: multiply_side(OWN, 0, 0)],
        (3, 0): [lambda: multiply_side(HOP1, 0, 0), lambda: y_finish(0, 1)],
        (3, 1): [lambda: multiply_side(OWN, 0, 1), lambda: forward(1, 2)],
        (3, 2): [lambda: multiply_side(HOP1, 0, 1), lambda: forward(1, 3)],
        (3, 3): [lambda: multiply_side(HOP2, 0, 0), lambda: sum_cores(OWN)],
        (3, 4): [lambda: multiply_side(HOP2, 0, 1)],
        (3, 5): [lambda: sum_cores(HOP1)],
        (3, 6): [lambda: sum_cores(HOP2)],
    }
    for hop in range(1, 4):
        for sub in range(8):
            z_step(hop, sub)
            for action in after.get((hop, sub), ()):
                action()
    multiply_urgent(HOP3)
    y_finish(1, 0)
    multiply_side(OWN, 1, 0)
    multiply_side(HOP1, 1, 0)
    sum_cores(HOP3)
    y_finish(1, 1)
    multiply_side(OWN, 1, 1)
    multiply_side(HOP1, 1, 1)
    multiply(HOP2, 1)
    sum_chips(OWN)
    sum_chips(HOP1)
    for sub in range(8):
        z_wait(sub // 4, 4, sub)
    multiply_urgent(LAST)
    multiply(HOP3, 1)
    sum_cores(LAST)
    multiply(LAST, 1)
    for group in (HOP2, HOP3, LAST):
        sum_chips(group)
    for p in range(8):

        @pl.when(jnp.logical_not(stays(p)))
        def _():
            for chunk in range(CHUNKS):
                a_copy(chunk, p, False).wait_send()

    for chunk in range(CHUNKS):
        x_opposite(chunk, True).wait_send()
        x_partner(chunk, True).wait_send()
    for first in range(2):
        for chunk in range(CHUNKS):
            for way in range(2):
                y_copy(way, first, chunk).wait_send()
            forward_copy(first, chunk).wait_send()
    for way in range(2):
        for hop in range(4):
            for sub in range(8):
                if hop < 3 or sub // 4 == way:
                    z_copy(way, hop, sub).wait_send()
    for group in GROUPS:
        for first in range(2):
            peer_copy(group, first).wait_send()
        half_copy(group).wait_send()


def on_device(snapshots, cell_weight):
    hbm = pl.BlockSpec(memory_space=pltpu.HBM)
    dma = pltpu.SemaphoreType.DMA
    return pl.pallas_call(
        kernel,
        out_shape=jax.ShapeDtypeStruct((2 * SNAP, COLS), jnp.float32),
        in_specs=[hbm, hbm],
        out_specs=pl.BlockSpec(memory_space=pltpu.VMEM),
        scratch_shapes=[
            pltpu.VMEM((SNAP, CELL), jnp.bfloat16),
            pltpu.VMEM((CELL,), jnp.float32),
            pltpu.VMEM((SNAP, CELL), jnp.bfloat16),
            pltpu.VMEM((SNAP, CELL), jnp.bfloat16),
            pltpu.VMEM((2 * SNAP, 4 * CELL), jnp.bfloat16),
            pltpu.VMEM((8 * PIECE, 4 * CELL), jnp.bfloat16),
            pltpu.VMEM((2, 2, 8 * PIECE, COLS), jnp.float32),
            pltpu.VMEM((2, 8 * PIECE, COLS), jnp.float32),
            pltpu.VMEM((8 * PIECE, COLS), jnp.bfloat16),
            pltpu.VMEM((8 * PIECE, COLS), jnp.bfloat16),
            dma((2,)),
            dma((CHUNKS, 8)), dma((CHUNKS, 8)),
            dma((CHUNKS,)), dma((2, CHUNKS)), dma((2, CHUNKS)),
            dma((2, 2, CHUNKS)), dma((2, 2, CHUNKS)),
            dma((2, CHUNKS)), dma((2, CHUNKS)),
            dma((2, 4, 8)), dma((2, 4, 8)),
            dma((2, 6)), dma((2, 6)), dma((6,)), dma((6,)),
        ],
        compiler_params=pltpu.CompilerParams(
            collective_id=0, has_side_effects=True, vmem_limit_bytes=40 << 20
        ),
        name="gram",
    )(pltpu.with_memory_space_constraint(snapshots, pltpu.HBM), pltpu.with_memory_space_constraint(cell_weight, pltpu.HBM))


def solution(mesh):
    return jax.shard_map(
        on_device,
        mesh=mesh,
        in_specs=(P("col", ("row", "depth")), P(("row", "depth"))),
        out_specs=P("row", ("col", "depth")),
        check_vma=False,
    )
```
